32 devices in a mesh: phase: 2 (over core), expert: 4 (over z), dp: 4 (over y, x).
Axes of the slice: x: 2, y: 2, z: 4, core: 2. Of those that a mesh axis runs over, the one named last changes fastest.
Arguments:
- fwd_in: bfloat16 [2, 256, 16, 1024], P('phase', ('expert', 'dp')), may hold values from -6 to 6
- saved_in: bfloat16 [2, 256, 16, 1024], P('phase', ('expert', 'dp')), may hold values from -6 to 6
- upstream: bfloat16 [2, 256, 16, 1024], P('phase', ('expert', 'dp')), may hold values from -6 to 6
- routes: int32 [2, 2, 256, 2], P('phase', None, ('expert', 'dp')), may hold values from 0 to 3, all different within a row; in each aligned block of 16 rows (0 to 15, 16 to 31, ..., all dimensions but the last counted through in order) at most 16 rows name the same one
- gates: float32 [2, 2, 256, 2], P('phase', None, ('expert', 'dp')), may hold values from 0.25 to 1
- capacity: int32 [2, 4], P('phase'), may hold values from 1 to 16
- dilation_log: int32 [2, 4], P('phase'), may hold values from 0 to 2
- conv_kernel: bfloat16 [2, 4, 3, 1024], P('phase', 'expert'), may hold values from -3.5 to 3.5
- up_weight: bfloat16 [2, 4, 1024, 2048], P('phase', 'expert'), may hold values from -0.1875 to 0.1875
- down_weight: bfloat16 [2, 4, 2048, 1024], P('phase', 'expert'), may hold values from -0.125 to 0.125
Outputs:
- passed: bfloat16 [2, 256, 16, 1024], P('phase', ('expert', 'dp'))
- finished: bfloat16 [2, 256, 16, 1024], P('phase', ('expert', 'dp'))
- up_grad: bfloat16 [2, 4, 1024, 2048], P('phase', 'expert', 'dp')
- down_grad: bfloat16 [2, 4, 2048, 1024], P('phase', 'expert', 'dp')
- kernel_grad: float32 [2, 4, 3, 1024], P('phase', 'expert', None, 'dp')
The draws below stay inside these ranges and needn't reach their ends.
Inputs may be any that keep to these rules, and one draw needn't show every extreme that they name: `routes`: each row names 2 different experts. Within the rows of one device (aligned blocks of 16 tiles) no expert is named by more than 16 tiles, a bound that some block reaches.
All inputs are finite; a program needn't handle non-finite values.
Results may differ from the reference program's by a relative error of at most 0.013.
Values may be sent and summed in bfloat16 or wider, within the bound.
A program may use at most 128 MiB of HBM per device.

```python
import math
import jax
import jax.numpy as jnp
import numpy as np
from jax import lax

D = 1024
FF = 2048
STEPS = 16
TAPS = 3
TOP = 2
TILES_DEV = 16
RIM = 8
EXPERTS = 4
CAP = 16
TILES = 256
N_DP = 4


def place_ends(result, stream_key, smallest, high):
    longest = result.shape.index(max(result.shape))
    spots = []
    for shift in (0, 1):
        where = [jax.random.randint(jax.random.fold_in(stream_key, axis), (), 0, length) for axis, length in enumerate(result.shape)]
        where[longest] = (where[longest] + shift) % result.shape[longest]
        spots.append(tuple(where))
    return result.at[spots[0]].set(smallest).at[spots[1]].set(high)


def level_of(rng, extent, shards, low, high):
    def one(axis_at, shards_of):
        heights = jax.random.uniform(jax.random.fold_in(jax.random.fold_in(rng, 6), axis_at), (shards_of,), jnp.float32, low / len(shards), high / len(shards))
        return jnp.repeat(jnp.exp(heights), extent[axis_at] // shards_of).reshape((-1,) + (1,) * (len(extent) - axis_at - 1))

    factor_of = one(*shards[0])
    for cut in shards[1:]:
        factor_of = factor_of * one(*cut)
    return factor_of


def shared_out(stream_key, own, number, rows, amount, top, reach, skew):
    order = jax.random.permutation(stream_key, amount)
    heavy_load, common = load_shares(amount, rows * top, reach, skew, True), load_shares(amount, rows * top, reach, skew, False)
    places = jnp.arange(amount)

    def named(sizes, turn):
        used = int((sizes > 0).sum())
        fixed = max(1, used // 4)
        shifted = fixed + (places - fixed + turn * (used - fixed)) % max(1, amount - fixed)
        return jnp.zeros((amount,), jnp.int32).at[order[jnp.where(places < fixed, places, shifted)]].set(jnp.asarray(sizes, jnp.int32))

    sizes = jnp.where(number % 4 == 0, named(heavy_load, number // 4), named(common, number - number // 4 - 1))
    mixed = jax.random.permutation(jax.random.fold_in(own, 3), amount)
    donor, taker = mixed[0:amount // 2 * 2:2], mixed[1:amount // 2 * 2:2]
    margin = jnp.minimum(sizes[donor] - 1, reach - sizes[taker]) // 2
    margin = jnp.where((donor == order[0]) | (taker == order[0]) | (sizes[taker] == 0), 0, jnp.maximum(margin, 0))
    shifted = jax.random.randint(jax.random.fold_in(own, 4), (amount // 2,), 0, 1 << 20) % (margin + 1)
    sizes = sizes.at[donor].add(-shifted).at[taker].add(shifted)
    labels = jnp.searchsorted(jnp.cumsum(sizes), jnp.arange(rows * top), side="right").astype(jnp.int32)
    table = labels.reshape(top, rows).T
    table = table[jax.random.permutation(jax.random.fold_in(own, 1), rows)]
    turn = jax.random.randint(jax.random.fold_in(own, 2), (rows, 1), 0, top)
    return jnp.take_along_axis(table, (jnp.arange(top)[None, :] + turn) % top, axis=1)


def load_shares(amount, total, most, skew, full):
    loads = [(1 << 20) // math.isqrt(rank ** skew) + 1 for rank in range(1, amount + 1)]
    largest = most if full else min(most, max(-(-total // amount), total * loads[0] // sum(loads)))
    least = 1 if total - largest >= amount - 1 else 0
    given, spare = [largest] + [least] * (amount - 1), total - largest - least * (amount - 1)
    while spare > 0:
        movable = [i for i in range(1, amount) if given[i] < largest] or [i for i in range(1, amount) if given[i] < most]
        pool, left = sum([loads[i] for i in movable]), spare
        for i in movable:
            more = min(most - given[i], max(1, left * loads[i] // pool), spare)
            given[i] = given[i] + more
            spare = spare - more
    return np.array(given)


def noise(key, dims, spread, reach, split=(), held_as=jnp.bfloat16):
    values = spread * jax.random.normal(key, dims, jnp.float32)
    if split:
        values = values * level_of(key, dims, split, -0.22, 0.18)
    return jnp.clip(values, -reach, reach).astype(held_as)


def setup_inputs(seed: int = 0) -> dict:
    splits = jax.random.split(jax.random.key(seed), 11)
    fwd_in = noise(splits[0], (2, TILES, STEPS, D), 1.0, 6.0, ((0, 2), (1, 16)))
    saved_in = noise(splits[1], (2, TILES, STEPS, D), 1.0, 6.0, ((0, 2), (1, 16)))
    upstream = noise(splits[2], (2, TILES, STEPS, D), 1.0, 6.0, ((0, 2), (1, 16)))
    routes_keys = jax.random.split(jax.random.fold_in(splits[3], 1), 2 * 2 * TILES // TILES_DEV)
    routes_turns = jax.random.permutation(jax.random.fold_in(splits[3], 3), 2 * 2 * TILES // TILES_DEV)
    routes = jax.vmap(lambda own, number: shared_out(jax.random.fold_in(splits[3], 2), own, number, TILES_DEV, EXPERTS, TOP, CAP, 2))(routes_keys, routes_turns).reshape((2, 2, TILES, TOP))
    gates = jnp.clip(0.25 + 0.75 * jax.random.uniform(splits[4], (2, 2, TILES, TOP), jnp.float32) ** level_of(splits[4], (2, 2, TILES, TOP), ((0, 2), (2, 16)), -0.2, 0.2), 0.25, 1.0)
    capacity = place_ends(jax.random.randint(splits[5], (2, EXPERTS), 1, CAP + 1), jax.random.fold_in(splits[5], 1), 1, CAP).astype(jnp.int32)
    dilation_log = place_ends(jax.random.randint(splits[6], (2, EXPERTS), 0, 3), jax.random.fold_in(splits[6], 1), 0, 2).astype(jnp.int32)
    conv_kernel = noise(splits[7], (2, EXPERTS, TAPS, D), TAPS ** -0.5, 3.5, ((0, 2), (1, 4)))
    up_weight = noise(splits[8], (2, EXPERTS, D, FF), D ** -0.5, 0.1875, ((0, 2), (1, 4)))
    down_weight = noise(splits[9], (2, EXPERTS, FF, D), FF ** -0.5, 0.125, ((0, 2), (1, 4)))
    return {"fwd_in": fwd_in, "saved_in": saved_in, "upstream": upstream, "routes": routes, "gates": gates, "capacity": capacity, "dilation_log": dilation_log, "conv_kernel": conv_kernel, "up_weight": up_weight, "down_weight": down_weight}


grad_scale = 0.0625

def gelu_and_slope(pre_act):
    primal, pull_back = jax.vjp(lambda operand: jax.nn.gelu(operand, approximate=True), pre_act)
    return (primal, pull_back(jnp.ones_like(pre_act))[0])

def tap_hits(dilations):
    offsets = jnp.arange(TAPS, dtype=jnp.int32)[None, :] * dilations[:, None]
    return offsets[:, :, None] == jnp.arange(RIM + 1, dtype=jnp.int32)[None, None, :]

def offset_table(kernels, dilations):
    hits_all = tap_hits(dilations)
    return lax.optimization_barrier(jnp.sum(jnp.where(hits_all[:, :, :, None], kernels[:, :, None, :].astype(jnp.float32), 0.0), axis=1))

def fold_taps(lagged, dilations):
    hits_all = tap_hits(dilations)
    return lax.optimization_barrier(jnp.sum(jnp.where(hits_all[:, :, :, None], lagged[:, None, :, :], 0.0), axis=2))

def causal_mix(tile_rows, tap_table):
    length = tile_rows.shape[1]
    padded = jnp.pad(tile_rows, ((0, 0), (RIM, 0), (0, 0)))
    summed = jnp.zeros(tile_rows.shape, jnp.float32)
    for offset in range(RIM + 1):
        summed = summed + padded[:, RIM - offset:RIM - offset + length].astype(jnp.float32) * tap_table[:, offset][:, None, :]
    return summed

def anti_mix(grad_rows, tap_table):
    length = grad_rows.shape[1]
    padded = jnp.pad(grad_rows, ((0, 0), (0, RIM), (0, 0)))
    summed = jnp.zeros(grad_rows.shape, jnp.float32)
    for offset in range(RIM + 1):
        summed = summed + padded[:, offset:offset + length].astype(jnp.float32) * tap_table[:, offset][:, None, :]
    return summed

def lag_products(grad_rows, tile_rows):
    length = tile_rows.shape[1]
    padded = jnp.pad(tile_rows, ((0, 0), (RIM, 0), (0, 0)))
    lagged = []
    for offset in range(RIM + 1):
        lagged.append(lax.optimization_barrier(jnp.sum(grad_rows.astype(jnp.float32) * padded[:, RIM - offset:RIM - offset + length].astype(jnp.float32), axis=1)))
    return jnp.stack(lagged, axis=1)

def copy_plan(route_rows, limits, dilations):
    blocks = route_rows.reshape(TILES // TILES_DEV, TILES_DEV * TOP)
    tile_place = jnp.arange(TILES_DEV * TOP, dtype=jnp.int32) // TOP
    matching = blocks[:, :, None] == blocks[:, None, :]
    earlier = tile_place[None, :] < tile_place[:, None]
    ranking = lax.optimization_barrier(jnp.sum(jnp.where(matching & earlier[None], 1, 0), axis=2)).reshape(-1).astype(jnp.int32)
    expert_ids = route_rows.reshape(-1)
    named = expert_ids[:, None] == jnp.arange(EXPERTS, dtype=jnp.int32)[None, :]
    allowed = lax.optimization_barrier(jnp.sum(jnp.where(named, limits[None, :], 0), axis=1))
    copy_span = lax.optimization_barrier(jnp.sum(jnp.where(named, dilations[None, :], 0), axis=1))
    return (expert_ids, ranking < allowed, copy_span)

def layer_forward(tile_rows, route_rows, gate_rows, limits, dilations, kernels, up_matrix, down_matrix):
    expert_ids, kept, copy_span = copy_plan(route_rows, limits, dilations)
    tap_table = offset_table(kernels[expert_ids], copy_span)
    mixed = causal_mix(jnp.repeat(tile_rows, TOP, axis=0), tap_table).astype(jnp.bfloat16)

    def apply_expert(element):
        conv_rows, expert = element
        pre_act = jnp.dot(conv_rows, up_matrix[expert], preferred_element_type=jnp.float32)
        hidden = jax.nn.gelu(pre_act, approximate=True).astype(jnp.bfloat16)
        return jnp.dot(hidden, down_matrix[expert], preferred_element_type=jnp.float32).astype(jnp.bfloat16)
    expert_rows = lax.map(apply_expert, (mixed, expert_ids))
    weights = gate_rows.reshape(-1) * kept.astype(jnp.float32)
    branch = lax.optimization_barrier(jnp.sum((expert_rows.astype(jnp.float32) * weights[:, None, None]).reshape(TILES, TOP, STEPS, D), axis=1))
    return (tile_rows.astype(jnp.float32) + branch).astype(jnp.bfloat16)

def layer_backward(tile_rows, route_rows, gate_rows, limits, dilations, kernels, up_matrix, down_matrix, incoming):
    expert_ids, kept, copy_span = copy_plan(route_rows, limits, dilations)
    tap_table = offset_table(kernels[expert_ids], copy_span)
    copy_rows = jnp.repeat(tile_rows, TOP, axis=0)
    mixed = causal_mix(copy_rows, tap_table).astype(jnp.bfloat16)
    weights = gate_rows.reshape(-1) * kept.astype(jnp.float32)
    grad_rows = (weights[:, None, None] * jnp.repeat(incoming, TOP, axis=0).astype(jnp.float32)).astype(jnp.bfloat16)
    copy_total = TILES * TOP
    sort_key = jnp.where(kept, expert_ids, EXPERTS).astype(jnp.int32)
    sorted_copies = jnp.argsort(sort_key, stable=True).astype(jnp.int32)
    counts = lax.optimization_barrier(jnp.sum(jnp.where(sort_key[None, :] == jnp.arange(EXPERTS, dtype=jnp.int32)[:, None], 1, 0), axis=1)).astype(jnp.int32)
    starts = (jnp.cumsum(counts) - counts).astype(jnp.int32)
    group_of = jnp.arange(copy_total, dtype=jnp.int32) // TOP // TILES_DEV % N_DP

    def per_expert(conv_grads, expert):

        def one_copy(position, carried):
            conv_grads, up_part, down_part = carried
            copy_id = sorted_copies[starts[expert] + position]
            conv_rows = mixed[copy_id]
            grad_here = grad_rows[copy_id]
            pre_act = jnp.dot(conv_rows, up_matrix[expert], preferred_element_type=jnp.float32)
            hidden, slopes = gelu_and_slope(pre_act)
            hidden = hidden.astype(jnp.bfloat16)
            hidden_grad = jnp.dot(grad_here, down_matrix[expert].T, preferred_element_type=jnp.float32)
            pre_grad = (hidden_grad * slopes).astype(jnp.bfloat16)
            conv_grad = jnp.dot(pre_grad, up_matrix[expert].T, preferred_element_type=jnp.float32).astype(jnp.bfloat16)
            group_id = group_of[copy_id]
            up_part = up_part.at[group_id].add(jnp.dot(conv_rows.T, pre_grad, preferred_element_type=jnp.float32))
            down_part = down_part.at[group_id].add(jnp.dot(hidden.T, grad_here, preferred_element_type=jnp.float32))
            conv_grads = conv_grads.at[copy_id].set(conv_grad)
            return (conv_grads, up_part, down_part)
        initial = (conv_grads, jnp.zeros((N_DP, D, FF), jnp.float32), jnp.zeros((N_DP, FF, D), jnp.float32))
        conv_grads, up_part, down_part = lax.fori_loop(0, counts[expert], one_copy, initial)
        up_round = lax.optimization_barrier(up_part.astype(jnp.bfloat16)).astype(jnp.float32)
        down_round = lax.optimization_barrier(down_part.astype(jnp.bfloat16)).astype(jnp.float32)
        up_total = (lax.optimization_barrier(jnp.sum(up_round, axis=0)) * grad_scale).astype(jnp.bfloat16)
        down_total = (lax.optimization_barrier(jnp.sum(down_round, axis=0)) * grad_scale).astype(jnp.bfloat16)
        return (conv_grads, (up_total, down_total))
    conv_grads, (up_grads, down_grads) = lax.scan(per_expert, jnp.zeros((copy_total, STEPS, D), jnp.bfloat16), jnp.arange(EXPERTS, dtype=jnp.int32))
    tile_grads = anti_mix(conv_grads, tap_table).astype(jnp.bfloat16)
    in_grad = (incoming.astype(jnp.float32) + lax.optimization_barrier(jnp.sum(tile_grads.astype(jnp.float32).reshape(TILES, TOP, STEPS, D), axis=1))).astype(jnp.bfloat16)
    per_copy = fold_taps(lag_products(conv_grads, copy_rows), copy_span)
    kernel_grads = jax.ops.segment_sum(per_copy, expert_ids, num_segments=EXPERTS) * grad_scale
    return (in_grad, up_grads, down_grads, kernel_grads)

def reference(fwd_in, saved_in, upstream, routes, gates, capacity, dilation_log, conv_kernel, up_weight, down_weight):
    dilations = jnp.left_shift(jnp.ones_like(dilation_log), dilation_log)
    layer_outs = []
    in_grads = []
    up_list = []
    down_list = []
    kernel_list = []
    for section in range(2):
        layer_outs.append(layer_forward(fwd_in[section], routes[section, 0], gates[section, 0], capacity[section], dilations[section], conv_kernel[section], up_weight[section], down_weight[section]))
        in_grad, up_grads, down_grads, kernel_grads = layer_backward(saved_in[section], routes[section, 1], gates[section, 1], capacity[section], dilations[section], conv_kernel[section], up_weight[section], down_weight[section], upstream[section])
        in_grads.append(in_grad)
        up_list.append(up_grads)
        down_list.append(down_grads)
        kernel_list.append(kernel_grads)
    passed = jnp.stack([in_grads[1], layer_outs[0]])
    finished = jnp.stack([in_grads[0], layer_outs[1]])
    return (passed, finished, jnp.stack(up_list), jnp.stack(down_list), jnp.stack(kernel_list))
```

```python
import functools
import math

import jax
import jax.numpy as jnp
from jax import lax
from jax.experimental import pallas as pl
from jax.experimental.pallas import tpu as pltpu
from jax.sharding import PartitionSpec as P

TAPS = 3
TOP = 2
RIM = 8
LANES = 128
PART = 512
CHUNK = 64
HALVES = 2
ROOT = math.sqrt(2.0 / math.pi)
CUBIC = 0.044715
VMEM_BYTES = 62 * 1024 * 1024
MESH = pl.DeviceIdType.MESH


grad_scale = 0.0625


def from_behind(block, axis, distance):
    devices = range(lax.axis_size(axis))
    route = [(i - distance, i) for i in devices if i - distance in devices]
    return lax.ppermute(block, axis, route)


def gelu_and_slope(pre_act):
    primal, pull_back = jax.vjp(lambda operand: jax.nn.gelu(operand, approximate=True), pre_act)
    return (primal, pull_back(jnp.ones_like(pre_act))[0])


def tap_hits(dilations):
    offsets = jnp.arange(TAPS, dtype=jnp.int32)[None, :] * dilations[:, None]
    return offsets[:, :, None] == jnp.arange(RIM + 1, dtype=jnp.int32)[None, None, :]


def offset_table(kernels, dilations):
    hits_all = tap_hits(dilations)
    return jnp.sum(
        jnp.where(hits_all[:, :, :, None], kernels[:, :, None, :].astype(jnp.float32), 0.0), axis=1
    )


def fold_taps(lagged, dilations):
    hits_all = tap_hits(dilations)
    return jnp.sum(jnp.where(hits_all[:, :, :, None], lagged[:, None, :, :], 0.0), axis=2)


def causal_mix(tile_rows, tap_table):
    length = tile_rows.shape[1]
    padded = jnp.pad(tile_rows, ((0, 0), (RIM, 0), (0, 0)))
    summed = jnp.zeros(tile_rows.shape, jnp.float32)
    for offset in range(RIM + 1):
        summed = (
            summed
            + padded[:, RIM - offset : RIM - offset + length].astype(jnp.float32)
            * tap_table[:, offset][:, None, :]
        )
    return summed


def anti_mix(grad_rows, tap_table):
    length = grad_rows.shape[1]
    padded = jnp.pad(grad_rows, ((0, 0), (0, RIM), (0, 0)))
    summed = jnp.zeros(grad_rows.shape, jnp.float32)
    for offset in range(RIM + 1):
        summed = (
            summed
            + padded[:, offset : offset + length].astype(jnp.float32)
            * tap_table[:, offset][:, None, :]
        )
    return summed


def lag_products(grad_rows, tile_rows):
    length = tile_rows.shape[1]
    padded = jnp.pad(tile_rows, ((0, 0), (RIM, 0), (0, 0)))
    lagged = []
    for offset in range(RIM + 1):
        lagged.append(
            jnp.sum(
                grad_rows.astype(jnp.float32)
                * padded[:, RIM - offset : RIM - offset + length].astype(jnp.float32),
                axis=1,
            )
        )
    return jnp.stack(lagged, axis=1)


def slot_plan(route_rows, limits, dilations, slot_depth):
    experts_all = limits.shape[0]
    expert_ids = route_rows.reshape(-1)
    copies = expert_ids.shape[0]
    tile_place = jnp.arange(copies, dtype=jnp.int32) // TOP
    matching = expert_ids[:, None] == expert_ids[None, :]
    earlier = tile_place[None, :] < tile_place[:, None]
    ranking = jnp.sum(jnp.where(matching & earlier, 1, 0), axis=1).astype(jnp.int32)
    named = expert_ids[:, None] == jnp.arange(experts_all, dtype=jnp.int32)[None, :]
    allowed = jnp.sum(jnp.where(named, limits[None, :], 0), axis=1)
    copy_span = jnp.sum(jnp.where(named, dilations[None, :], 0), axis=1)
    return (expert_ids, ranking < allowed, expert_ids * slot_depth + ranking, copy_span)


def select_rows(source_rows, row_index, live_rows):
    total, steps, channels = source_rows.shape
    chosen = (row_index[:, None] == jnp.arange(total, dtype=jnp.int32)[None, :]) & live_rows[
        :, None
    ]
    picked = jnp.dot(
        chosen.astype(source_rows.dtype),
        source_rows.reshape(total, steps * channels),
        preferred_element_type=jnp.float32,
    )
    return picked.astype(source_rows.dtype).reshape(-1, steps, channels)


def pack_slots(source_rows, source_index, kept, slot_index, slot_total):
    matching = (slot_index[None, :] == jnp.arange(slot_total, dtype=jnp.int32)[:, None]) & kept[
        None, :
    ]
    filled = jnp.any(matching, axis=1)
    chosen = jnp.sum(jnp.where(matching, source_index[None, :], 0), axis=1)
    return (select_rows(source_rows, chosen, filled), filled)


def compact_plan(filled):
    live_int = filled.astype(jnp.int32)
    targets = jnp.arange(filled.shape[0], dtype=jnp.int32)
    before = targets[None, :] < targets[:, None]
    position = jnp.sum(jnp.where(before, live_int[None, :], 0), axis=1)
    live_count = jnp.sum(live_int)
    matching = (position[None, :] == targets[:, None]) & filled[None, :]
    picked = jnp.sum(jnp.where(matching, targets[None, :], 0), axis=1)
    return (picked, position, live_count, targets < live_count)


def owner_forward(mixed, live_count, up_matrix, down_matrix):
    slot_total, tile_steps, channels = mixed.shape
    block_slots = math.gcd(slot_total, 16)
    rounds = (live_count + block_slots - 1) // block_slots

    def one_block(number, results):
        inputs = lax.dynamic_slice_in_dim(mixed, number * block_slots, block_slots, 0).reshape(
            block_slots * tile_steps, channels
        )
        pre_act = jnp.dot(inputs, up_matrix, preferred_element_type=jnp.float32)
        hidden = jax.nn.gelu(pre_act, approximate=True).astype(jnp.bfloat16)
        outputs = jnp.dot(hidden, down_matrix, preferred_element_type=jnp.float32).astype(
            jnp.bfloat16
        )
        return lax.dynamic_update_slice_in_dim(
            results, outputs.reshape(block_slots, tile_steps, channels), number * block_slots, 0
        )

    return lax.fori_loop(0, rounds, one_block, jnp.zeros_like(mixed))


def owner_backward(mixed, grad_out, live_count, up_matrix, down_matrix):
    slot_total, tile_steps, channels = mixed.shape
    block_slots = math.gcd(slot_total, 16)
    rounds = (live_count + block_slots - 1) // block_slots
    last_dims = (((1,), (1,)), ((), ()))
    first_dims = (((0,), (0,)), ((), ()))

    def one_block(number, carried):
        up_sum, down_sum, conv_grads = carried
        inputs = lax.dynamic_slice_in_dim(mixed, number * block_slots, block_slots, 0).reshape(
            block_slots * tile_steps, channels
        )
        grad_here = lax.dynamic_slice_in_dim(
            grad_out, number * block_slots, block_slots, 0
        ).reshape(block_slots * tile_steps, channels)
        pre_act = jnp.dot(inputs, up_matrix, preferred_element_type=jnp.float32)
        hidden, slopes = gelu_and_slope(pre_act)
        hidden = hidden.astype(jnp.bfloat16)
        hidden_grad = lax.dot_general(
            grad_here, down_matrix, last_dims, preferred_element_type=jnp.float32
        )
        pre_grad = (hidden_grad * slopes).astype(jnp.bfloat16)
        input_grad = lax.dot_general(
            pre_grad, up_matrix, last_dims, preferred_element_type=jnp.float32
        ).astype(jnp.bfloat16)
        up_sum = up_sum + lax.dot_general(
            inputs, pre_grad, first_dims, preferred_element_type=jnp.float32
        )
        down_sum = down_sum + lax.dot_general(
            hidden, grad_here, first_dims, preferred_element_type=jnp.float32
        )
        conv_grads = lax.dynamic_update_slice_in_dim(
            conv_grads,
            input_grad.reshape(block_slots, tile_steps, channels),
            number * block_slots,
            0,
        )
        return (up_sum, down_sum, conv_grads)

    initial = (
        jnp.zeros(up_matrix.shape, jnp.float32),
        jnp.zeros(down_matrix.shape, jnp.float32),
        jnp.zeros_like(mixed),
    )
    return lax.fori_loop(0, rounds, one_block, initial)


def local_slots(
    fwd_in,
    saved_in,
    upstream,
    routes,
    gates,
    capacity,
    dilation_log,
    conv_kernel,
    up_weight,
    down_weight,
):
    front_rows = fwd_in[0]
    saved_rows = saved_in[0]
    incoming = upstream[0]
    tile_count, tile_steps, channels = front_rows.shape
    experts = capacity.shape[1]
    slot_depth = 2 * max(1, (tile_count * TOP + experts - 1) // experts)
    slot_total = experts * slot_depth
    up_matrix = up_weight[0, 0]
    down_matrix = down_weight[0, 0]
    limits = capacity[0]
    dilations = jnp.left_shift(jnp.ones_like(dilation_log[0]), dilation_log[0])
    expert_front, kept_front, slot_front, span_front = slot_plan(
        routes[0, 0], limits, dilations, slot_depth
    )
    expert_saved, kept_saved, slot_saved, span_saved = slot_plan(
        routes[0, 1], limits, dilations, slot_depth
    )
    copies = expert_front.shape[0]
    every_copy = jnp.arange(copies, dtype=jnp.int32)
    tile_of = every_copy // TOP
    front_weights = gates[0, 0].reshape(-1) * kept_front.astype(jnp.float32)
    grad_copies = (
        gates[0, 1].reshape(-1)[:, None, None]
        * jnp.repeat(incoming, TOP, axis=0).astype(jnp.float32)
    ).astype(jnp.bfloat16)
    own_expert = lax.axis_index("expert")
    own_span = jnp.sum(
        jnp.where(jnp.arange(experts, dtype=jnp.int32) == own_expert, dilations, 0)
    ).reshape(1)
    own_table = offset_table(conv_kernel[0], own_span)
    send_front, filled_front = pack_slots(front_rows, tile_of, kept_front, slot_front, slot_total)
    got_front, flags_front = (
        lax.all_to_all(send_front, "expert", split_axis=0, concat_axis=0, tiled=True),
        lax.all_to_all(
            filled_front.astype(jnp.bfloat16), "expert", split_axis=0, concat_axis=0, tiled=True
        ),
    )
    live_front = flags_front > 0
    pick_front, place_front, count_front, dense_live_front = compact_plan(live_front)
    dense_front = select_rows(got_front, pick_front, dense_live_front)
    dense_front = causal_mix(dense_front, own_table).astype(jnp.bfloat16)
    results_front = owner_forward(dense_front, count_front, up_matrix, down_matrix)
    back_front = lax.all_to_all(
        select_rows(results_front, place_front, live_front),
        "expert",
        split_axis=0,
        concat_axis=0,
        tiled=True,
    )
    expert_rows = select_rows(back_front, slot_front, kept_front)
    branch = jnp.sum(
        (expert_rows.astype(jnp.float32) * front_weights[:, None, None]).reshape(
            tile_count, TOP, tile_steps, channels
        ),
        axis=1,
    )
    layer_out = (front_rows.astype(jnp.float32) + branch).astype(jnp.bfloat16)
    send_saved, filled_saved = pack_slots(saved_rows, tile_of, kept_saved, slot_saved, slot_total)
    send_grads, unused_flags = pack_slots(
        grad_copies, every_copy, kept_saved, slot_saved, slot_total
    )
    got_saved, got_grads, flags_saved = (
        lax.all_to_all(send_saved, "expert", split_axis=0, concat_axis=0, tiled=True),
        lax.all_to_all(send_grads, "expert", split_axis=0, concat_axis=0, tiled=True),
        lax.all_to_all(
            filled_saved.astype(jnp.bfloat16), "expert", split_axis=0, concat_axis=0, tiled=True
        ),
    )
    live_saved = flags_saved > 0
    pick_saved, place_saved, count_saved, dense_live_saved = compact_plan(live_saved)
    dense_saved = select_rows(got_saved, pick_saved, dense_live_saved)
    dense_grads = select_rows(got_grads, pick_saved, dense_live_saved)
    mixed_dense = causal_mix(dense_saved, own_table).astype(jnp.bfloat16)
    up_sum, down_sum, conv_grads = owner_backward(
        mixed_dense, dense_grads, count_saved, up_matrix, down_matrix
    )
    outgoing = anti_mix(conv_grads, own_table).astype(jnp.bfloat16)
    lagged = jnp.sum(lag_products(conv_grads, dense_saved), axis=0, keepdims=True)
    kernel_local = (
        lax.psum_scatter(fold_taps(lagged, own_span)[0], "dp", scatter_dimension=1, tiled=True)
        * grad_scale
    )
    back_saved = lax.all_to_all(
        select_rows(outgoing, place_saved, live_saved),
        "expert",
        split_axis=0,
        concat_axis=0,
        tiled=True,
    )
    copy_grads = select_rows(back_saved, slot_saved, kept_saved)
    layer_in_grad = (
        incoming.astype(jnp.float32)
        + jnp.sum(
            copy_grads.astype(jnp.float32).reshape(tile_count, TOP, tile_steps, channels), axis=1
        )
    ).astype(jnp.bfloat16)
    up_part, down_part = (
        lax.psum_scatter(up_sum.astype(jnp.bfloat16), "dp", scatter_dimension=0, tiled=True).astype(
            jnp.float32
        ),
        lax.psum_scatter(
            down_sum.astype(jnp.bfloat16), "dp", scatter_dimension=0, tiled=True
        ).astype(jnp.float32),
    )
    up_grad = (up_part * grad_scale).astype(jnp.bfloat16)
    down_grad = (down_part * grad_scale).astype(jnp.bfloat16)
    upper_section = lax.axis_index("phase") == 1
    came_up = from_behind(layer_out, "phase", 1)
    came_down = from_behind(layer_in_grad, "phase", -1)
    passed = jnp.where(upper_section, came_up, came_down)
    finished = jnp.where(upper_section, layer_out, layer_in_grad)
    return (
        passed[None],
        finished[None],
        up_grad[None, None],
        down_grad[None, None],
        kernel_local[None, None],
    )


def tile_weights(route_rows, gate_rows, limits):
    named = route_rows[..., None] == jnp.arange(limits.shape[0], dtype=jnp.int32)
    by_tile = jnp.any(named, axis=2).astype(jnp.int32)
    places = jnp.arange(route_rows.shape[1], dtype=jnp.int32)
    earlier = (places[None, :] < places[:, None]).astype(jnp.int32)
    ranking = jnp.sum(earlier[None, :, :, None] * by_tile[:, None, :, :], axis=2)
    gate_of = jnp.sum(jnp.where(named, gate_rows[..., None], 0.0), axis=2)
    weights = jnp.where(ranking < limits, gate_of, 0.0).transpose(0, 2, 1)
    return jnp.broadcast_to(weights[..., None], weights.shape + (LANES,))


def fill_shifts(shifts, dilation, rows, steps):
    row = lax.broadcasted_iota(jnp.int32, (rows, rows), 0)
    column = lax.broadcasted_iota(jnp.int32, (rows, rows), 1)
    same = row // steps == column // steps
    for place_at, gap in enumerate((row - column, column - row)):
        for j in (1, 2):
            hit = jnp.where((gap == j * dilation) & same, 1.0, 0.0)
            shifts[2 * place_at + j - 1] = hit.astype(jnp.bfloat16)


def mm(a, b, dims=((1,), (0,))):
    return lax.dot_general(a, b, (dims, ((), ())), preferred_element_type=jnp.float32)


def widen(weight_row, channels):
    return jnp.concatenate([weight_row] * (channels // LANES), axis=1)


def gelu_parts(x):
    square = x * x
    bend = jnp.tanh(x * (ROOT + ROOT * CUBIC * square))
    half = 0.5 * (1.0 + bend)
    slope = half + 0.5 * x * (1.0 - bend * bend) * (ROOT + 3.0 * ROOT * CUBIC * square)
    return x * half, slope


def place(me, k):
    distance = (k + 1) // 2
    return me + (1 - 2 * (k % 2)) * distance


def greet(me, n, phase, others):
    barrier = pltpu.get_barrier_semaphore()
    for valid, beside in [(me > 0, me - 1), (me < n - 1, me + 1)]:
        @pl.when(valid)
        def _():
            for device in ({"expert": beside}, {"phase": 1 - phase, "expert": beside}):
                pl.semaphore_signal(barrier, inc=1, device_id=device, device_id_type=MESH)
    for device in others:
        pl.semaphore_signal(barrier, inc=1, device_id=device, device_id_type=MESH)


def greeted(me, n, others):
    barrier = pltpu.get_barrier_semaphore()
    inner = (me > 0) & (me < n - 1)

    @pl.when(inner)
    def _():
        pl.semaphore_wait(barrier, len(others) + 4)

    @pl.when(jnp.logical_not(inner))
    def _():
        pl.semaphore_wait(barrier, len(others) + 2)


def within(n, block):
    return (block >= 0) & (block < n)


def gather_copies(block, slot, target, half, buffers, send_sems, recv_sems):
    copies = []
    for t, buffer in enumerate(buffers):
        if t < len(buffers) - 1:
            extent = buffer.shape[1] // HALVES
            view = buffer.at[block, pl.ds(half * extent, extent)]
        elif half == 0:
            view = buffer.at[block]
        else:
            continue
        copies.append(
            pltpu.make_async_remote_copy(
                src_ref=view,
                dst_ref=view,
                send_sem=send_sems.at[slot, half, t],
                recv_sem=recv_sems.at[slot, half, t],
                device_id={"expert": target},
                device_id_type=MESH,
            )
        )
    return copies


def take_in(n, me, k, half, buffers, send_sems, recv_sems, arrived):
    block = place(me, k)
    outward = 2 * (k % 2) - 1
    target = me + outward

    @pl.when(within(n, block))
    def _():
        for copy in gather_copies(block, k, me - outward, half, buffers, send_sems, recv_sems):
            copy.wait_recv()

        @pl.when(within(n, target))
        def _():
            for copy in gather_copies(block, k + 2, target, half, buffers, send_sems, recv_sems):
                copy.start()

        arrived(block, k, half, outward)


def take_ring(n, me, distance, half, way, arrived):
    @pl.when(distance < n)
    def _():
        take_in(n, me, 2 * distance - 1, half, *way, arrived)
        take_in(n, me, 2 * distance, half, *way, arrived)


def own_send(n, me, direction, buffers, send_sems, recv_sems, start=True):
    target = me + 1 - 2 * direction

    @pl.when(within(n, target))
    def _():
        for half in range(HALVES):
            for copy in gather_copies(
                me, 1 + direction, target, half, buffers, send_sems, recv_sems
            ):
                if start:
                    copy.start()
                else:
                    copy.wait_send()


def drain_gather(n, me, buffers, send_sems, recv_sems):
    for direction in (0, 1):
        own_send(n, me, direction, buffers, send_sems, recv_sems, False)

    def step(k, carry):
        block = place(me, k)
        target = me + 2 * (k % 2) - 1

        @pl.when(within(n, block) & within(n, target))
        def _():
            for half in range(HALVES):
                for copy in gather_copies(
                    block, k + 2, target, half, buffers, send_sems, recv_sems
                ):
                    copy.wait_send()

        return carry

    lax.fori_loop(1, 2 * n - 1, step, 0)


def home_copy(dir_index, half, source, landing, sends, recvs, dest, target):
    extent = source.shape[1] // HALVES
    rows = pl.ds(half * extent, extent)
    return pltpu.make_async_remote_copy(
        src_ref=source.at[dest, rows],
        dst_ref=landing.at[dir_index, dest, rows],
        send_sem=sends.at[dest, half],
        recv_sem=recvs.at[dir_index, dest, half],
        device_id={"expert": target},
        device_id_type=MESH,
    )


def home_first(n, me, k, way):
    dir_index = k % 2
    sign = 1 - 2 * dir_index

    @pl.when((k > 0) & jnp.logical_not(within(n, me - sign)))
    def _():
        for half in range(HALVES):
            home_copy(dir_index, half, *way, place(me, k), me + sign).start()


def home_rest(n, me, way):
    source, landing = way[:2]
    extent = source.shape[1] // HALVES
    turned = me // (n // 2)

    def step(r, carry):
        dir_index = (r // (n - 1) + turned) % 2
        sign = 1 - 2 * dir_index
        dest = me + sign * (r % (n - 1) + 1)

        @pl.when(within(n, dest) & within(n, me - sign))
        def _():
            for half in range(HALVES):
                rows = slice(half * extent, (half + 1) * extent)
                home_copy(dir_index, half, *way, dest, me - sign).wait_recv()
                source[dest, rows, :] = (
                    source[dest, rows, :].astype(jnp.float32)
                    + landing[dir_index, dest, rows, :].astype(jnp.float32)
                ).astype(jnp.bfloat16)
                home_copy(dir_index, half, *way, dest, me + sign).start()

        return carry

    lax.fori_loop(0, 2 * n - 2, step, 0)


def home_sent(n, me, way):
    def step(k, carry):
        dest = place(me, k)
        ahead = me + 1 - 2 * (k % 2)

        @pl.when(within(n, dest))
        def _():
            for half in range(HALVES):
                home_copy(k % 2, half, *way, dest, ahead).wait_send()

        return carry

    lax.fori_loop(1, 2 * n - 1, step, 0)


def step_kernel(
    n, ndp, tiles, steps,
    front_hbm, saved_hbm, upstream_hbm, weights_hbm, dilation_ref,
    kernel_ref, up_hbm, down_hbm,
    passed_hbm, finished_hbm, up_grad_hbm, down_grad_hbm, taps_out_ref,
    front, saved, incoming, weights_front, weights_back, shifts, taps, up, down,
    mixed, grads, hidden, pre_grads, one_back, two_back, total,
    results, up_part, tile_grad, land_back, land_front, down_part, up_land, down_land,
    taps_grad, taps_land,
    local_sems, saved_send, saved_recv, front_send, front_recv,
    home_front_send, home_front_recv, home_back_send, home_back_recv,
    up_send, up_recv, down_send, down_recv, taps_send, taps_recv, swap_sems, turns,
):
    me = lax.axis_index("expert")
    lane = lax.axis_index("dp")
    phase = lax.axis_index("phase")
    rows = tiles * steps
    channels = front.shape[2]
    width = up.shape[1]
    loads = [
        pltpu.make_async_copy(saved_hbm, saved.at[me], local_sems.at[0]),
        pltpu.make_async_copy(upstream_hbm, incoming.at[me], local_sems.at[1]),
        pltpu.make_async_copy(up_hbm, up, local_sems.at[3]),
        pltpu.make_async_copy(down_hbm, down, local_sems.at[4]),
        pltpu.make_async_copy(front_hbm, front.at[me], local_sems.at[2]),
    ]
    loads[2:2] = [
        pltpu.make_async_copy(weights_hbm.at[1], weights_back.at[me], local_sems.at[8]),
        pltpu.make_async_copy(weights_hbm.at[0], weights_front.at[me], local_sems.at[9]),
    ]
    for load in loads:
        load.start()
    x_lane = lane // 2 * 2 + (1 - lane % 2)
    y_lane = (1 - lane // 2) * 2 + lane % 2
    far_lane = (1 - lane // 2) * 2 + (1 - lane % 2)
    peers = [x_lane, y_lane, far_lane]
    others = [{"dp": peer} for peer in peers] + [{"phase": 1 - phase}]
    greet(me, n, phase, others)
    greeted(me, n, others)
    for load in loads[:3]:
        load.wait()
    back_way = ((saved, incoming, weights_back), saved_send, saved_recv)
    front_way = ((front, weights_front), front_send, front_recv)
    back_home = (tile_grad, land_back, home_back_send, home_back_recv)
    front_home = (results, land_front, home_front_send, home_front_recv)
    front_mixed = one_back
    out_front, out_back = two_back, one_back
    edge = (me == 0) | (me == n - 1)

    @pl.when(phase == 0)
    def _():
        for direction in (0, 1):
            own_send(n, me, direction, *back_way)

    taps_grad[...] = jnp.zeros_like(taps_grad)
    taps[0:TAPS, :] = kernel_ref[...].astype(jnp.float32)
    fill_shifts(shifts, jnp.left_shift(1, dilation_ref[0, me]), rows, steps)
    for load in loads[3:]:
        load.wait()

    def work_back(block):
        here = pl.ds(pl.multiple_of(block * rows, rows), rows)

        x = saved[block]
        x1 = mm(shifts[0], x)
        x2 = mm(shifts[1], x)
        one_back[...] = x1.astype(jnp.bfloat16)
        two_back[...] = x2.astype(jnp.bfloat16)
        mixed[here, :] = (
            x.astype(jnp.float32) * taps[0:1, :] + x1 * taps[1:2, :] + x2 * taps[2:3, :]
        ).astype(jnp.bfloat16)
        for t in range(tiles):
            weight = widen(weights_back[block, me, t : t + 1, :], channels)
            tile = incoming[block, t * steps : (t + 1) * steps, :].astype(jnp.float32)
            grads[pl.ds(pl.multiple_of(block * rows + t * steps, steps), steps), :] = (
                weight * tile
            ).astype(jnp.bfloat16)
        total[...] = jnp.zeros_like(total)

        def part(f, carry):
            there = pl.ds(pl.multiple_of(f * PART, PART), PART)
            pre_act = mm(mixed[here, :], up[:, there])
            hidden_grad = mm(grads[here, :], down[there, :], ((1,), (1,)))
            primal, slope = gelu_parts(pre_act)
            hidden[here, there] = primal.astype(jnp.bfloat16)
            pre_grad = (hidden_grad * slope).astype(jnp.bfloat16)
            pre_grads[here, there] = pre_grad
            total[...] += mm(pre_grad, up[:, there], ((1,), (1,)))
            return carry

        lax.fori_loop(0, width // PART, part, 0)
        conv_grad = total[...].astype(jnp.bfloat16)
        wide = conv_grad.astype(jnp.float32)
        tile_grad[block] = (
            wide * taps[0:1, :]
            + mm(shifts[2], conv_grad) * taps[1:2, :]
            + mm(shifts[3], conv_grad) * taps[2:3, :]
        ).astype(jnp.bfloat16)
        for j, source in enumerate((saved.at[block], one_back, two_back)):
            taps_grad[j : j + 1, :] += jnp.sum(
                wide * source[...].astype(jnp.float32), axis=0, keepdims=True
            )

    def work_front(block):
        x = front[block]
        front_mixed[...] = (
            x.astype(jnp.float32) * taps[0:1, :]
            + mm(shifts[0], x) * taps[1:2, :]
            + mm(shifts[1], x) * taps[2:3, :]
        ).astype(jnp.bfloat16)
        total[...] = jnp.zeros_like(total)

        def part(f, carry):
            there = pl.ds(pl.multiple_of(f * PART, PART), PART)
            pre_act = mm(front_mixed[...], up[:, there])
            hidden = gelu_parts(pre_act)[0].astype(jnp.bfloat16)
            total[...] += mm(hidden, down[there, :])
            return carry

        lax.fori_loop(0, width // PART, part, 0)
        for t in range(tiles):
            weight = widen(weights_front[block, me, t : t + 1, :], channels)
            here = slice(t * steps, (t + 1) * steps)
            expert_rows = total[here, :].astype(jnp.bfloat16).astype(jnp.float32)
            results[block, here, :] = (weight * expert_rows).astype(jnp.bfloat16)

    def give_turn(at, outward):
        pl.semaphore_signal(
            turns.at[at],
            inc=1,
            device_id={"phase": 1 - phase, "expert": me - outward},
            device_id_type=MESH,
        )

    def last_block(block, k):
        return block == (n - 1) * (1 - k % 2)

    def back_arrived(block, k, half, outward):
        @pl.when((phase == half) & last_block(block, k))
        def _():
            give_turn(1 - k % 2, outward)

    def front_arrived(block, k, half, outward):
        if half == 0:
            @pl.when((phase == 0) & last_block(block, k))
            def _():
                give_turn(3 - k % 2, outward)

    def await_turn(first, send):
        for i in (0, 1):
            direction = (i + me // (n // 2)) % 2

            @pl.when(within(n, me + 1 - 2 * direction))
            def _():
                pl.semaphore_wait(turns.at[first + direction], 1)

            send(direction)

    def back_step(k, carry):
        distance = (k + 1) // 2
        block = place(me, k)

        @pl.when(within(n, block))
        def _():
            work_back(block)
            home_first(n, me, k, back_home)

        @pl.when(k == 0)
        def _():
            @pl.when(phase == 1)
            def _():
                work_front(me)
                await_turn(0, lambda direction: own_send(n, me, direction, *back_way))

            take_ring(n, me, 1, 0, back_way, back_arrived)
            take_ring(n, me, 1, 1, back_way, back_arrived)

        @pl.when((k == 0) & (phase == 0) & edge)
        def _():
            for direction in (0, 1):
                own_send(n, me, direction, *front_way)

        @pl.when(k % 2 == 1)
        def _():
            take_ring(n, me, distance + 1, 0, back_way, back_arrived)

        @pl.when((k % 2 == 0) & (k > 0))
        def _():
            take_ring(n, me, distance + 1, 1, back_way, back_arrived)

        return carry

    lax.fori_loop(0, 2 * n - 1, back_step, 0)

    def down_rows(piece, dest):
        def rows_of(i, carry):
            extent = down_land.shape[1]
            there = pl.ds(pl.multiple_of(dest * extent + i * 256, 256), 256)
            here = pl.ds(pl.multiple_of(i * 256, 256), 256)
            down_part[piece, here, :] = mm(hidden[:, there], grads[...], ((0,), (0,))).astype(jnp.bfloat16)
            return carry

        lax.fori_loop(0, down_land.shape[1] // 256, rows_of, 0)

    def up_rows(piece, dest):
        def rows_of(i, carry):
            extent = up_land.shape[1]
            there = pl.ds(pl.multiple_of(dest * extent + i * 256, 256), 256)
            here = pl.ds(pl.multiple_of(i * 256, 256), 256)
            up_part[piece, here, :] = mm(mixed[:, there], pre_grads[...], ((0,), (0,))).astype(jnp.bfloat16)
            return carry

        lax.fori_loop(0, up_land.shape[1] // 256, rows_of, 0)

    def share(part, land, sends, recvs, slot, target):
        return pltpu.make_async_remote_copy(
            src_ref=part.at[slot],
            dst_ref=land.at[slot],
            send_sem=sends.at[slot],
            recv_sem=recvs.at[slot],
            device_id={"dp": target},
            device_id_type=MESH,
        )

    def pass_on(part, land, sends, recvs, target):
        return pltpu.make_async_remote_copy(
            src_ref=part.at[2],
            dst_ref=land.at[2],
            send_sem=sends.at[2],
            recv_sem=recvs.at[2],
            device_id={"dp": target},
            device_id_type=MESH,
        )

    def relay(part, land, copies, hop):
        copies[0].wait_recv()

        def add(i, carry):
            there = pl.ds(pl.multiple_of(i * CHUNK, CHUNK), CHUNK)
            part[2, there, :] = (
                land[0, there, :].astype(jnp.float32) + part[2, there, :].astype(jnp.float32)
            ).astype(jnp.bfloat16)
            return carry

        lax.fori_loop(0, land.shape[1] // CHUNK, add, 0)
        hop.start()

    def arrive(part, land, copies, hop, out, sem):
        copies[1].wait_recv()
        hop.wait_recv()

        def add(i, carry):
            there = pl.ds(pl.multiple_of(i * CHUNK, CHUNK), CHUNK)
            summed = (
                part[3, there, :].astype(jnp.float32)
                + land[1, there, :].astype(jnp.float32)
                + land[2, there, :].astype(jnp.float32)
            )
            part[3, there, :] = (summed * grad_scale).astype(jnp.bfloat16)
            return carry

        lax.fori_loop(0, land.shape[1] // CHUNK, add, 0)
        store = pltpu.make_async_copy(part.at[3], out, sem)
        store.start()
        return store

    down_copies = [
        share(down_part, down_land, down_send, down_recv, 0, y_lane),
        share(down_part, down_land, down_send, down_recv, 1, y_lane),
    ]
    up_copies = [
        share(up_part, up_land, up_send, up_recv, 0, x_lane),
        share(up_part, up_land, up_send, up_recv, 1, x_lane),
    ]
    down_rows(0, far_lane)
    down_copies[0].start()
    up_rows(0, far_lane)
    up_copies[0].start()
    down_rows(1, y_lane)
    down_copies[1].start()
    up_rows(1, x_lane)
    up_copies[1].start()
    tap_copies = [
        pltpu.make_async_remote_copy(
            src_ref=taps_grad.at[pl.ds(0, 8), pl.ds(pl.multiple_of(peer * tap_share, tap_share), tap_share)],
            dst_ref=taps_land.at[j],
            send_sem=taps_send.at[j],
            recv_sem=taps_recv.at[j],
            device_id={"dp": peer},
            device_id_type=MESH,
        )
        for tap_share in (taps_land.shape[2],)
        for j, peer in enumerate(peers)
    ]
    for copy in tap_copies:
        copy.start()

    down_rows(2, x_lane)
    up_rows(2, y_lane)
    down_hop = pass_on(down_part, down_land, down_send, down_recv, x_lane)
    up_hop = pass_on(up_part, up_land, up_send, up_recv, y_lane)
    down_rows(3, lane)
    up_rows(3, lane)
    relay(down_part, down_land, down_copies, down_hop)
    relay(up_part, up_land, up_copies, up_hop)
    home_rest(n, me, back_home)

    @pl.when(phase == 0)
    def _():
        def send(direction):
            @pl.when(jnp.logical_not(edge))
            def _():
                own_send(n, me, direction, *front_way)

        await_turn(0, send)

    @pl.when(phase == 1)
    def _():
        await_turn(2, lambda direction: own_send(n, me, direction, *front_way))

    def front_step(k, carry):
        distance = (k + 1) // 2
        block = place(me, k)

        @pl.when(within(n, block) & ((k > 0) | (phase == 0)))
        def _():
            work_front(block)
            home_first(n, me, k, front_home)

        @pl.when(k == 0)
        def _():
            take_ring(n, me, 1, 0, front_way, front_arrived)
            take_ring(n, me, 1, 1, front_way, front_arrived)

        @pl.when(k % 2 == 1)
        def _():
            take_ring(n, me, distance + 1, 0, front_way, front_arrived)

        @pl.when((k % 2 == 0) & (k > 0))
        def _():
            take_ring(n, me, distance + 1, 1, front_way, front_arrived)

        return carry

    lax.fori_loop(0, 2 * n - 1, front_step, 0)

    def settle(way, resid, out):
        source, landing = way[:2]
        for dir_index in (0, 1):
            behind = me - (1 - 2 * dir_index)

            @pl.when(within(n, behind))
            def _():
                for half in range(HALVES):
                    home_copy(dir_index, half, *way, me, behind).wait_recv()

        out[...] = resid.astype(jnp.float32) + source[me].astype(jnp.float32)
        for dir_index in (0, 1):
            behind = me - (1 - 2 * dir_index)

            @pl.when((behind >= 0) & (behind < n))
            def _():
                out[...] += landing[dir_index, me].astype(jnp.float32)

    def swap(source):
        return pltpu.make_async_remote_copy(
            src_ref=source,
            dst_ref=passed_hbm,
            send_sem=swap_sems.at[0],
            recv_sem=swap_sems.at[1],
            device_id={"phase": 1 - phase},
            device_id_type=MESH,
        )

    def finish(source):
        return pltpu.make_async_copy(source, finished_hbm, local_sems.at[7])

    settle(back_home, incoming[me], total)
    out_back[...] = total[...].astype(jnp.bfloat16)

    @pl.when(phase == 0)
    def _():
        finish(out_back).start()

    @pl.when(phase == 1)
    def _():
        swap(out_back).start()

    stores = [
        arrive(down_part, down_land, down_copies, down_hop, down_grad_hbm, local_sems.at[5]),
        arrive(up_part, up_land, up_copies, up_hop, up_grad_hbm, local_sems.at[6]),
    ]
    for copy in tap_copies:
        copy.wait()
    tap_share = taps_land.shape[2]
    taps_sum = taps_grad[:, pl.ds(pl.multiple_of(lane * tap_share, tap_share), tap_share)]
    for j in range(ndp - 1):
        taps_sum = taps_sum + taps_land[j]
    taps_out_ref[...] = taps_sum * grad_scale
    home_rest(n, me, front_home)
    settle(front_home, front[me], total)
    out_front[...] = total[...].astype(jnp.bfloat16)

    @pl.when(phase == 0)
    def _():
        swap(out_front).start()

    @pl.when(phase == 1)
    def _():
        finish(out_front).start()

    drain_gather(n, me, *back_way)
    drain_gather(n, me, *front_way)
    home_sent(n, me, back_home)
    home_sent(n, me, front_home)
    for copy in down_copies + up_copies + [down_hop, up_hop]:
        copy.wait_send()
    for store in stores:
        store.wait()

    @pl.when(phase == 0)
    def _():
        finish(out_back).wait()

    @pl.when(phase == 1)
    def _():
        finish(out_front).wait()

    swap(out_front).wait()


def deliver_kernel(*refs):
    count = len(refs) // 2
    for i in range(count - 1):
        refs[count + i][...] = refs[i][...]
    taps_in, taps_out = refs[count - 1], refs[-1]
    taps_out[0, 0] = taps_in[: taps_out.shape[2], :]


def local_gather(
    fwd_in, saved_in, upstream, routes, gates, capacity, dilation_log, conv_kernel,
    up_weight, down_weight,
):
    n = lax.axis_size("expert")
    ndp = lax.axis_size("dp")
    _, tiles, steps, channels = fwd_in.shape
    width = up_weight.shape[3]
    rows = tiles * steps
    flat, every = (rows, channels), (n, rows, channels)
    bf16, f32 = jnp.bfloat16, jnp.float32
    vmem, anywhere = pl.BlockSpec(memory_space=pltpu.VMEM), pl.BlockSpec(memory_space=pl.ANY)
    smem = pl.BlockSpec(memory_space=pltpu.SMEM)
    slots = 2 * n + 1
    up_share, down_share, tap_share = channels // ndp, width // ndp, channels // ndp
    dma = pltpu.SemaphoreType.DMA
    out_shape = (
        jax.ShapeDtypeStruct(flat, bf16),
        jax.ShapeDtypeStruct(flat, bf16),
        jax.ShapeDtypeStruct((up_share, width), bf16),
        jax.ShapeDtypeStruct((down_share, channels), bf16),
        jax.ShapeDtypeStruct((8, tap_share), f32),
    )
    outs = pl.pallas_call(
        functools.partial(step_kernel, n, ndp, tiles, steps),
        out_shape=out_shape,
        in_specs=[anywhere] * 4 + [smem, vmem, anywhere, anywhere],
        out_specs=(anywhere, anywhere, anywhere, anywhere, vmem),
        scratch_shapes=[
            pltpu.VMEM(every, bf16),
            pltpu.VMEM(every, bf16),
            pltpu.VMEM(every, bf16),
            pltpu.VMEM((n, n, tiles, LANES), f32),
            pltpu.VMEM((n, n, tiles, LANES), f32),
            pltpu.VMEM((4, rows, rows), bf16),
            pltpu.VMEM((8, channels), f32),
            pltpu.VMEM((channels, width), bf16),
            pltpu.VMEM((width, channels), bf16),
            pltpu.VMEM((n * rows, channels), bf16),
            pltpu.VMEM((n * rows, channels), bf16),
            pltpu.VMEM((n * rows, width), bf16),
            pltpu.VMEM((n * rows, width), bf16),
            pltpu.VMEM(flat, bf16),
            pltpu.VMEM(flat, bf16),
            pltpu.VMEM(flat, f32),
            pltpu.VMEM(every, bf16),
            pltpu.VMEM((ndp, up_share, width), bf16),
            pltpu.VMEM(every, bf16),
            pltpu.VMEM((2,) + every, bf16),
            pltpu.VMEM((2,) + every, bf16),
            pltpu.VMEM((ndp, down_share, channels), bf16),
            pltpu.VMEM((3, up_share, width), bf16),
            pltpu.VMEM((3, down_share, channels), bf16),
            pltpu.VMEM((8, channels), f32),
            pltpu.VMEM((ndp - 1, 8, tap_share), f32),
            dma((10,)),
            dma((slots, HALVES, 3)),
            dma((slots, HALVES, 3)),
            dma((slots, HALVES, 2)),
            dma((slots, HALVES, 2)),
            dma((n, HALVES)),
            dma((2, n, HALVES)),
            dma((n, HALVES)),
            dma((2, n, HALVES)),
            dma((3,)),
            dma((3,)),
            dma((3,)),
            dma((3,)),
            dma((ndp - 1,)),
            dma((ndp - 1,)),
            dma((2,)),
            pltpu.SemaphoreType.REGULAR((4,)),
        ],
        compiler_params=pltpu.CompilerParams(
            collective_id=0, has_side_effects=True, vmem_limit_bytes=VMEM_BYTES
        ),
    )(
        fwd_in.reshape(flat), saved_in.reshape(flat), upstream.reshape(flat),
        tile_weights(routes[0], gates[0], capacity[0]), dilation_log, conv_kernel[0, 0], up_weight[0, 0], down_weight[0, 0],
    )
    pieces = [
        pl.BlockSpec((out.shape[0] // 2, out.shape[1]), lambda i: (i, 0)) for out in out_shape[:4]
    ]
    taps_shape = jax.ShapeDtypeStruct((1, 1, TAPS, tap_share), f32)
    passed, finished, up_grad, down_grad, taps_out = pl.pallas_call(
        deliver_kernel,
        grid=(2,),
        out_shape=out_shape[:4] + (taps_shape,),
        in_specs=pieces + [pl.BlockSpec(out_shape[4].shape, lambda i: (0, 0))],
        out_specs=tuple(pieces) + (pl.BlockSpec(taps_shape.shape, lambda i: (0, 0, 0, 0)),),
    )(*outs)
    shape = fwd_in.shape
    return (
        passed.reshape(shape),
        finished.reshape(shape),
        up_grad[None, None],
        down_grad[None, None],
        taps_out,
    )


def local(*operands):
    tile_count, experts = operands[0].shape[1], operands[5].shape[1]
    slot_total = experts * 2 * max(1, (tile_count * TOP + experts - 1) // experts)
    gathers = experts * tile_count <= slot_total and lax.axis_size("dp") == 4
    return local_gather(*operands) if gathers else local_slots(*operands)


def solution(mesh):
    return jax.shard_map(
        local,
        mesh=mesh,
        in_specs=(
            P("phase", ("expert", "dp"), None, None),
            P("phase", ("expert", "dp"), None, None),
            P("phase", ("expert", "dp"), None, None),
            P("phase", None, ("expert", "dp"), None),
            P("phase", None, ("expert", "dp"), None),
            P("phase", None),
            P("phase", None),
            P("phase", "expert", None, None),
            P("phase", "expert", None, None),
            P("phase", "expert", None, None),
        ),
        out_specs=(
            P("phase", ("expert", "dp"), None, None),
            P("phase", ("expert", "dp"), None, None),
            P("phase", "expert", "dp", None),
            P("phase", "expert", "dp", None),
            P("phase", "expert", None, "dp"),
        ),
        check_vma=False,
    )
```

```python
import functools
import math

import jax
import jax.numpy as jnp
from jax import lax
from jax.experimental import pallas as pl
from jax.experimental.pallas import tpu as pltpu
from jax.sharding import PartitionSpec as P

TAPS = 3
TOP = 2
RIM = 8
LANES = 128
PART = 512
CHUNK = 64
HALVES = 2
ROOT = math.sqrt(2.0 / math.pi)
CUBIC = 0.044715
VMEM_BYTES = 62 * 1024 * 1024
MESH = pl.DeviceIdType.MESH


grad_scale = 0.0625


def from_behind(block, axis, distance):
    devices = range(lax.axis_size(axis))
    route = [(i - distance, i) for i in devices if i - distance in devices]
    return lax.ppermute(block, axis, route)


def gelu_and_slope(pre_act):
    primal, pull_back = jax.vjp(lambda operand: jax.nn.gelu(operand, approximate=True), pre_act)
    return (primal, pull_back(jnp.ones_like(pre_act))[0])


def tap_hits(dilations):
    offsets = jnp.arange(TAPS, dtype=jnp.int32)[None, :] * dilations[:, None]
    return offsets[:, :, None] == jnp.arange(RIM + 1, dtype=jnp.int32)[None, None, :]


def offset_table(kernels, dilations):
    hits_all = tap_hits(dilations)
    return jnp.sum(
        jnp.where(hits_all[:, :, :, None], kernels[:, :, None, :].astype(jnp.float32), 0.0), axis=1
    )


def fold_taps(lagged, dilations):
    hits_all = tap_hits(dilations)
    return jnp.sum(jnp.where(hits_all[:, :, :, None], lagged[:, None, :, :], 0.0), axis=2)


def causal_mix(tile_rows, tap_table):
    length = tile_rows.shape[1]
    padded = jnp.pad(tile_rows, ((0, 0), (RIM, 0), (0, 0)))
    summed = jnp.zeros(tile_rows.shape, jnp.float32)
    for offset in range(RIM + 1):
        summed = (
            summed
            + padded[:, RIM - offset : RIM - offset + length].astype(jnp.float32)
            * tap_table[:, offset][:, None, :]
        )
    return summed


def anti_mix(grad_rows, tap_table):
    length = grad_rows.shape[1]
    padded = jnp.pad(grad_rows, ((0, 0), (0, RIM), (0, 0)))
    summed = jnp.zeros(grad_rows.shape, jnp.float32)
    for offset in range(RIM + 1):
        summed = (
            summed
            + padded[:, offset : offset + length].astype(jnp.float32)
            * tap_table[:, offset][:, None, :]
        )
    return summed


def lag_products(grad_rows, tile_rows):
    length = tile_rows.shape[1]
    padded = jnp.pad(tile_rows, ((0, 0), (RIM, 0), (0, 0)))
    lagged = []
    for offset in range(RIM + 1):
        lagged.append(
            jnp.sum(
                grad_rows.astype(jnp.float32)
                * padded[:, RIM - offset : RIM - offset + length].astype(jnp.float32),
                axis=1,
            )
        )
    return jnp.stack(lagged, axis=1)


def slot_plan(route_rows, limits, dilations, slot_depth):
    experts_all = limits.shape[0]
    expert_ids = route_rows.reshape(-1)
    copies = expert_ids.shape[0]
    tile_place = jnp.arange(copies, dtype=jnp.int32) // TOP
    matching = expert_ids[:, None] == expert_ids[None, :]
    earlier = tile_place[None, :] < tile_place[:, None]
    ranking = jnp.sum(jnp.where(matching & earlier, 1, 0), axis=1).astype(jnp.int32)
    named = expert_ids[:, None] == jnp.arange(experts_all, dtype=jnp.int32)[None, :]
    allowed = jnp.sum(jnp.where(named, limits[None, :], 0), axis=1)
    copy_span = jnp.sum(jnp.where(named, dilations[None, :], 0), axis=1)
    return (expert_ids, ranking < allowed, expert_ids * slot_depth + ranking, copy_span)


def select_rows(source_rows, row_index, live_rows):
    total, steps, channels = source_rows.shape
    chosen = (row_index[:, None] == jnp.arange(total, dtype=jnp.int32)[None, :]) & live_rows[
        :, None
    ]
    picked = jnp.dot(
        chosen.astype(source_rows.dtype),
        source_rows.reshape(total, steps * channels),
        preferred_element_type=jnp.float32,
    )
    return picked.astype(source_rows.dtype).reshape(-1, steps, channels)


def pack_slots(source_rows, source_index, kept, slot_index, slot_total):
    matching = (slot_index[None, :] == jnp.arange(slot_total, dtype=jnp.int32)[:, None]) & kept[
        None, :
    ]
    filled = jnp.any(matching, axis=1)
    chosen = jnp.sum(jnp.where(matching, source_index[None, :], 0), axis=1)
    return (select_rows(source_rows, chosen, filled), filled)


def compact_plan(filled):
    live_int = filled.astype(jnp.int32)
    targets = jnp.arange(filled.shape[0], dtype=jnp.int32)
    before = targets[None, :] < targets[:, None]
    position = jnp.sum(jnp.where(before, live_int[None, :], 0), axis=1)
    live_count = jnp.sum(live_int)
    matching = (position[None, :] == targets[:, None]) & filled[None, :]
    picked = jnp.sum(jnp.where(matching, targets[None, :], 0), axis=1)
    return (picked, position, live_count, targets < live_count)


def owner_forward(mixed, live_count, up_matrix, down_matrix):
    slot_total, tile_steps, channels = mixed.shape
    block_slots = math.gcd(slot_total, 16)
    rounds = (live_count + block_slots - 1) // block_slots

    def one_block(number, results):
        inputs = lax.dynamic_slice_in_dim(mixed, number * block_slots, block_slots, 0).reshape(
            block_slots * tile_steps, channels
        )
        pre_act = jnp.dot(inputs, up_matrix, preferred_element_type=jnp.float32)
        hidden = jax.nn.gelu(pre_act, approximate=True).astype(jnp.bfloat16)
        outputs = jnp.dot(hidden, down_matrix, preferred_element_type=jnp.float32).astype(
            jnp.bfloat16
        )
        return lax.dynamic_update_slice_in_dim(
            results, outputs.reshape(block_slots, tile_steps, channels), number * block_slots, 0
        )

    return lax.fori_loop(0, rounds, one_block, jnp.zeros_like(mixed))


def owner_backward(mixed, grad_out, live_count, up_matrix, down_matrix):
    slot_total, tile_steps, channels = mixed.shape
    block_slots = math.gcd(slot_total, 16)
    rounds = (live_count + block_slots - 1) // block_slots
    last_dims = (((1,), (1,)), ((), ()))
    first_dims = (((0,), (0,)), ((), ()))

    def one_block(number, carried):
        up_sum, down_sum, conv_grads = carried
        inputs = lax.dynamic_slice_in_dim(mixed, number * block_slots, block_slots, 0).reshape(
            block_slots * tile_steps, channels
        )
        grad_here = lax.dynamic_slice_in_dim(
            grad_out, number * block_slots, block_slots, 0
        ).reshape(block_slots * tile_steps, channels)
        pre_act = jnp.dot(inputs, up_matrix, preferred_element_type=jnp.float32)
        hidden, slopes = gelu_and_slope(pre_act)
        hidden = hidden.astype(jnp.bfloat16)
        hidden_grad = lax.dot_general(
            grad_here, down_matrix, last_dims, preferred_element_type=jnp.float32
        )
        pre_grad = (hidden_grad * slopes).astype(jnp.bfloat16)
        input_grad = lax.dot_general(
            pre_grad, up_matrix, last_dims, preferred_element_type=jnp.float32
        ).astype(jnp.bfloat16)
        up_sum = up_sum + lax.dot_general(
            inputs, pre_grad, first_dims, preferred_element_type=jnp.float32
        )
        down_sum = down_sum + lax.dot_general(
            hidden, grad_here, first_dims, preferred_element_type=jnp.float32
        )
        conv_grads = lax.dynamic_update_slice_in_dim(
            conv_grads,
            input_grad.reshape(block_slots, tile_steps, channels),
            number * block_slots,
            0,
        )
        return (up_sum, down_sum, conv_grads)

    initial = (
        jnp.zeros(up_matrix.shape, jnp.float32),
        jnp.zeros(down_matrix.shape, jnp.float32),
        jnp.zeros_like(mixed),
    )
    return lax.fori_loop(0, rounds, one_block, initial)


def local_slots(
    fwd_in,
    saved_in,
    upstream,
    routes,
    gates,
    capacity,
    dilation_log,
    conv_kernel,
    up_weight,
    down_weight,
):
    front_rows = fwd_in[0]
    saved_rows = saved_in[0]
    incoming = upstream[0]
    tile_count, tile_steps, channels = front_rows.shape
    experts = capacity.shape[1]
    slot_depth = 2 * max(1, (tile_count * TOP + experts - 1) // experts)
    slot_total = experts * slot_depth
    up_matrix = up_weight[0, 0]
    down_matrix = down_weight[0, 0]
    limits = capacity[0]
    dilations = jnp.left_shift(jnp.ones_like(dilation_log[0]), dilation_log[0])
    expert_front, kept_front, slot_front, span_front = slot_plan(
        routes[0, 0], limits, dilations, slot_depth
    )
    expert_saved, kept_saved, slot_saved, span_saved = slot_plan(
        routes[0, 1], limits, dilations, slot_depth
    )
    copies = expert_front.shape[0]
    every_copy = jnp.arange(copies, dtype=jnp.int32)
    tile_of = every_copy // TOP
    front_weights = gates[0, 0].reshape(-1) * kept_front.astype(jnp.float32)
    grad_copies = (
        gates[0, 1].reshape(-1)[:, None, None]
        * jnp.repeat(incoming, TOP, axis=0).astype(jnp.float32)
    ).astype(jnp.bfloat16)
    own_expert = lax.axis_index("expert")
    own_span = jnp.sum(
        jnp.where(jnp.arange(experts, dtype=jnp.int32) == own_expert, dilations, 0)
    ).reshape(1)
    own_table = offset_table(conv_kernel[0], own_span)
    send_front, filled_front = pack_slots(front_rows, tile_of, kept_front, slot_front, slot_total)
    got_front, flags_front = (
        lax.all_to_all(send_front, "expert", split_axis=0, concat_axis=0, tiled=True),
        lax.all_to_all(
            filled_front.astype(jnp.bfloat16), "expert", split_axis=0, concat_axis=0, tiled=True
        ),
    )
    live_front = flags_front > 0
    pick_front, place_front, count_front, dense_live_front = compact_plan(live_front)
    dense_front = select_rows(got_front, pick_front, dense_live_front)
    dense_front = causal_mix(dense_front, own_table).astype(jnp.bfloat16)
    results_front = owner_forward(dense_front, count_front, up_matrix, down_matrix)
    back_front = lax.all_to_all(
        select_rows(results_front, place_front, live_front),
        "expert",
        split_axis=0,
        concat_axis=0,
        tiled=True,
    )
    expert_rows = select_rows(back_front, slot_front, kept_front)
    branch = jnp.sum(
        (expert_rows.astype(jnp.float32) * front_weights[:, None, None]).reshape(
            tile_count, TOP, tile_steps, channels
        ),
        axis=1,
    )
    layer_out = (front_rows.astype(jnp.float32) + branch).astype(jnp.bfloat16)
    send_saved, filled_saved = pack_slots(saved_rows, tile_of, kept_saved, slot_saved, slot_total)
    send_grads, unused_flags = pack_slots(
        grad_copies, every_copy, kept_saved, slot_saved, slot_total
    )
    got_saved, got_grads, flags_saved = (
        lax.all_to_all(send_saved, "expert", split_axis=0, concat_axis=0, tiled=True),
        lax.all_to_all(send_grads, "expert", split_axis=0, concat_axis=0, tiled=True),
        lax.all_to_all(
            filled_saved.astype(jnp.bfloat16), "expert", split_axis=0, concat_axis=0, tiled=True
        ),
    )
    live_saved = flags_saved > 0
    pick_saved, place_saved, count_saved, dense_live_saved = compact_plan(live_saved)
    dense_saved = select_rows(got_saved, pick_saved, dense_live_saved)
    dense_grads = select_rows(got_grads, pick_saved, dense_live_saved)
    mixed_dense = causal_mix(dense_saved, own_table).astype(jnp.bfloat16)
    up_sum, down_sum, conv_grads = owner_backward(
        mixed_dense, dense_grads, count_saved, up_matrix, down_matrix
    )
    outgoing = anti_mix(conv_grads, own_table).astype(jnp.bfloat16)
    lagged = jnp.sum(lag_products(conv_grads, dense_saved), axis=0, keepdims=True)
    kernel_local = (
        lax.psum_scatter(fold_taps(lagged, own_span)[0], "dp", scatter_dimension=1, tiled=True)
        * grad_scale
    )
    back_saved = lax.all_to_all(
        select_rows(outgoing, place_saved, live_saved),
        "expert",
        split_axis=0,
        concat_axis=0,
        tiled=True,
    )
    copy_grads = select_rows(back_saved, slot_saved, kept_saved)
    layer_in_grad = (
        incoming.astype(jnp.float32)
        + jnp.sum(
            copy_grads.astype(jnp.float32).reshape(tile_count, TOP, tile_steps, channels), axis=1
        )
    ).astype(jnp.bfloat16)
    up_part, down_part = (
        lax.psum_scatter(up_sum.astype(jnp.bfloat16), "dp", scatter_dimension=0, tiled=True).astype(
            jnp.float32
        ),
        lax.psum_scatter(
            down_sum.astype(jnp.bfloat16), "dp", scatter_dimension=0, tiled=True
        ).astype(jnp.float32),
    )
    up_grad = (up_part * grad_scale).astype(jnp.bfloat16)
    down_grad = (down_part * grad_scale).astype(jnp.bfloat16)
    upper_section = lax.axis_index("phase") == 1
    came_up = from_behind(layer_out, "phase", 1)
    came_down = from_behind(layer_in_grad, "phase", -1)
    passed = jnp.where(upper_section, came_up, came_down)
    finished = jnp.where(upper_section, layer_out, layer_in_grad)
    return (
        passed[None],
        finished[None],
        up_grad[None, None],
        down_grad[None, None],
        kernel_local[None, None],
    )


def fill_weights(passing, me, experts, routes, gates, capacity, weights):
    ranks = [jnp.int32(0)] * experts
    for t in range(routes.shape[2]):
        first, second = routes[passing, 0, t], routes[passing, 1, t]
        for e in range(experts):
            named = (first == e) | (second == e)
            gate = jnp.where(first == e, gates[passing, 0, t], gates[passing, 1, t])
            weight = jnp.where(named & (ranks[e] < capacity[0, e]), gate, 0.0)
            weights[me, e, t : t + 1, :] = jnp.full((1, LANES), weight, jnp.float32)
            ranks[e] = ranks[e] + jnp.where(named, 1, 0)


def fill_shifts(shifts, dilation, rows, steps):
    row = lax.broadcasted_iota(jnp.int32, (rows, rows), 0)
    column = lax.broadcasted_iota(jnp.int32, (rows, rows), 1)
    same = row // steps == column // steps
    for place_at, gap in enumerate((row - column, column - row)):
        for j in (1, 2):
            hit = jnp.where((gap == j * dilation) & same, 1.0, 0.0)
            shifts[2 * place_at + j - 1] = hit.astype(jnp.bfloat16)


def mm(a, b, dims=((1,), (0,))):
    return lax.dot_general(a, b, (dims, ((), ())), preferred_element_type=jnp.float32)


def widen(weight_row, channels):
    return jnp.concatenate([weight_row] * (channels // LANES), axis=1)


def gelu_parts(x):
    square = x * x
    bend = jnp.tanh(x * (ROOT + ROOT * CUBIC * square))
    half = 0.5 * (1.0 + bend)
    slope = half + 0.5 * x * (1.0 - bend * bend) * (ROOT + 3.0 * ROOT * CUBIC * square)
    return x * half, slope


def place(me, k):
    distance = (k + 1) // 2
    return me + (1 - 2 * (k % 2)) * distance


def greet(me, n, phase, others):
    barrier = pltpu.get_barrier_semaphore()
    for valid, beside in [(me > 0, me - 1), (me < n - 1, me + 1)]:
        @pl.when(valid)
        def _():
            for device in ({"expert": beside}, {"phase": 1 - phase, "expert": beside}):
                pl.semaphore_signal(barrier, inc=1, device_id=device, device_id_type=MESH)
    for device in others:
        pl.semaphore_signal(barrier, inc=1, device_id=device, device_id_type=MESH)


def greeted(me, n, others):
    barrier = pltpu.get_barrier_semaphore()
    inner = (me > 0) & (me < n - 1)

    @pl.when(inner)
    def _():
        pl.semaphore_wait(barrier, len(others) + 4)

    @pl.when(jnp.logical_not(inner))
    def _():
        pl.semaphore_wait(barrier, len(others) + 2)


def within(n, block):
    return (block >= 0) & (block < n)


def gather_copies(block, slot, target, half, buffers, send_sems, recv_sems):
    copies = []
    for t, buffer in enumerate(buffers):
        if t < len(buffers) - 1:
            extent = buffer.shape[1] // HALVES
            view = buffer.at[block, pl.ds(half * extent, extent)]
        elif half == 0:
            view = buffer.at[block]
        else:
            continue
        copies.append(
            pltpu.make_async_remote_copy(
                src_ref=view,
                dst_ref=view,
                send_sem=send_sems.at[slot, half, t],
                recv_sem=recv_sems.at[slot, half, t],
                device_id={"expert": target},
                device_id_type=MESH,
            )
        )
    return copies


def take_in(n, me, k, half, buffers, send_sems, recv_sems, arrived):
    block = place(me, k)
    outward = 2 * (k % 2) - 1
    target = me + outward

    @pl.when(within(n, block))
    def _():
        for copy in gather_copies(block, k, me - outward, half, buffers, send_sems, recv_sems):
            copy.wait_recv()

        @pl.when(within(n, target))
        def _():
            for copy in gather_copies(block, k + 2, target, half, buffers, send_sems, recv_sems):
                copy.start()

        arrived(block, k, half, outward)


def take_ring(n, me, distance, half, way, arrived):
    @pl.when(distance < n)
    def _():
        take_in(n, me, 2 * distance - 1, half, *way, arrived)
        take_in(n, me, 2 * distance, half, *way, arrived)


def own_send(n, me, direction, buffers, send_sems, recv_sems, start=True):
    target = me + 1 - 2 * direction

    @pl.when(within(n, target))
    def _():
        for half in range(HALVES):
            for copy in gather_copies(
                me, 1 + direction, target, half, buffers, send_sems, recv_sems
            ):
                if start:
                    copy.start()
                else:
                    copy.wait_send()


def drain_gather(n, me, buffers, send_sems, recv_sems):
    for direction in (0, 1):
        own_send(n, me, direction, buffers, send_sems, recv_sems, False)

    def step(k, carry):
        block = place(me, k)
        target = me + 2 * (k % 2) - 1

        @pl.when(within(n, block) & within(n, target))
        def _():
            for half in range(HALVES):
                for copy in gather_copies(
                    block, k + 2, target, half, buffers, send_sems, recv_sems
                ):
                    copy.wait_send()

        return carry

    lax.fori_loop(1, 2 * n - 1, step, 0)


def home_copy(dir_index, half, source, landing, sends, recvs, dest, target):
    extent = source.shape[1] // HALVES
    rows = pl.ds(half * extent, extent)
    return pltpu.make_async_remote_copy(
        src_ref=source.at[dest, rows],
        dst_ref=landing.at[dir_index, dest, rows],
        send_sem=sends.at[dest, half],
        recv_sem=recvs.at[dir_index, dest, half],
        device_id={"expert": target},
        device_id_type=MESH,
    )


def home_first(n, me, k, way):
    dir_index = k % 2
    sign = 1 - 2 * dir_index

    @pl.when((k > 0) & jnp.logical_not(within(n, me - sign)))
    def _():
        for half in range(HALVES):
            home_copy(dir_index, half, *way, place(me, k), me + sign).start()


def home_rest(n, me, way):
    source, landing = way[:2]
    extent = source.shape[1] // HALVES
    turned = me // (n // 2)

    def step(r, carry):
        dir_index = (r // (n - 1) + turned) % 2
        sign = 1 - 2 * dir_index
        dest = me + sign * (r % (n - 1) + 1)

        @pl.when(within(n, dest) & within(n, me - sign))
        def _():
            for half in range(HALVES):
                rows = slice(half * extent, (half + 1) * extent)
                home_copy(dir_index, half, *way, dest, me - sign).wait_recv()
                source[dest, rows, :] = (
                    source[dest, rows, :].astype(jnp.float32)
                    + landing[dir_index, dest, rows, :].astype(jnp.float32)
                ).astype(jnp.bfloat16)
                home_copy(dir_index, half, *way, dest, me + sign).start()

        return carry

    lax.fori_loop(0, 2 * n - 2, step, 0)


def home_sent(n, me, way):
    def step(k, carry):
        dest = place(me, k)
        ahead = me + 1 - 2 * (k % 2)

        @pl.when(within(n, dest))
        def _():
            for half in range(HALVES):
                home_copy(k % 2, half, *way, dest, ahead).wait_send()

        return carry

    lax.fori_loop(1, 2 * n - 1, step, 0)


def step_kernel(
    n, ndp, tiles, steps,
    front_hbm, saved_hbm, upstream_hbm, routes_ref, gates_ref, capacity_ref, dilation_ref,
    kernel_ref, up_hbm, down_hbm,
    passed_hbm, finished_hbm, up_grad_hbm, down_grad_hbm, taps_out_ref,
    front, saved, incoming, weights_front, weights_back, shifts, taps, up, down,
    mixed, grads, hidden, pre_grads, one_back, two_back, total,
    results, up_part, tile_grad, land_back, land_front, down_part, up_land, down_land,
    taps_grad, taps_land,
    local_sems, saved_send, saved_recv, front_send, front_recv,
    home_front_send, home_front_recv, home_back_send, home_back_recv,
    up_send, up_recv, down_send, down_recv, taps_send, taps_recv, swap_sems, turns,
):
    me = lax.axis_index("expert")
    lane = lax.axis_index("dp")
    phase = lax.axis_index("phase")
    rows = tiles * steps
    channels = front.shape[2]
    width = up.shape[1]
    loads = [
        pltpu.make_async_copy(saved_hbm, saved.at[me], local_sems.at[0]),
        pltpu.make_async_copy(upstream_hbm, incoming.at[me], local_sems.at[1]),
        pltpu.make_async_copy(up_hbm, up, local_sems.at[3]),
        pltpu.make_async_copy(down_hbm, down, local_sems.at[4]),
        pltpu.make_async_copy(front_hbm, front.at[me], local_sems.at[2]),
    ]
    for load in loads:
        load.start()
    x_lane = lane // 2 * 2 + (1 - lane % 2)
    y_lane = (1 - lane // 2) * 2 + lane % 2
    far_lane = (1 - lane // 2) * 2 + (1 - lane % 2)
    peers = [x_lane, y_lane, far_lane]
    others = [{"dp": peer} for peer in peers] + [{"phase": 1 - phase}]
    tables = (routes_ref, gates_ref, capacity_ref)
    fill_weights(1, me, n, *tables, weights_back)
    fill_weights(0, me, n, *tables, weights_front)
    greet(me, n, phase, others)
    greeted(me, n, others)
    for load in loads[:2]:
        load.wait()
    back_way = ((saved, incoming, weights_back), saved_send, saved_recv)
    front_way = ((front, weights_front), front_send, front_recv)
    back_home = (tile_grad, land_back, home_back_send, home_back_recv)
    front_home = (results, land_front, home_front_send, home_front_recv)
    front_mixed = one_back
    out_front, out_back = two_back, one_back
    edge = (me == 0) | (me == n - 1)

    @pl.when(phase == 0)
    def _():
        for direction in (0, 1):
            own_send(n, me, direction, *back_way)

    taps_grad[...] = jnp.zeros_like(taps_grad)
    taps[0:TAPS, :] = kernel_ref[...].astype(jnp.float32)
    fill_shifts(shifts, jnp.left_shift(1, dilation_ref[0, me]), rows, steps)
    for load in loads[2:]:
        load.wait()

    def work_back(block):
        here = pl.ds(pl.multiple_of(block * rows, rows), rows)

        x = saved[block]
        x1 = mm(shifts[0], x)
        x2 = mm(shifts[1], x)
        one_back[...] = x1.astype(jnp.bfloat16)
        two_back[...] = x2.astype(jnp.bfloat16)
        mixed[here, :] = (
            x.astype(jnp.float32) * taps[0:1, :] + x1 * taps[1:2, :] + x2 * taps[2:3, :]
        ).astype(jnp.bfloat16)
        for t in range(tiles):
            weight = widen(weights_back[block, me, t : t + 1, :], channels)
            tile = incoming[block, t * steps : (t + 1) * steps, :].astype(jnp.float32)
            grads[pl.ds(pl.multiple_of(block * rows + t * steps, steps), steps), :] = (
                weight * tile
            ).astype(jnp.bfloat16)
        total[...] = jnp.zeros_like(total)

        def part(f, carry):
            there = pl.ds(pl.multiple_of(f * PART, PART), PART)
            pre_act = mm(mixed[here, :], up[:, there])
            hidden_grad = mm(grads[here, :], down[there, :], ((1,), (1,)))
            primal, slope = gelu_parts(pre_act)
            hidden[here, there] = primal.astype(jnp.bfloat16)
            pre_grad = (hidden_grad * slope).astype(jnp.bfloat16)
            pre_grads[here, there] = pre_grad
            total[...] += mm(pre_grad, up[:, there], ((1,), (1,)))
            return carry

        lax.fori_loop(0, width // PART, part, 0)
        conv_grad = total[...].astype(jnp.bfloat16)
        wide = conv_grad.astype(jnp.float32)
        tile_grad[block] = (
            wide * taps[0:1, :]
            + mm(shifts[2], conv_grad) * taps[1:2, :]
            + mm(shifts[3], conv_grad) * taps[2:3, :]
        ).astype(jnp.bfloat16)
        for j, source in enumerate((saved.at[block], one_back, two_back)):
            taps_grad[j : j + 1, :] += jnp.sum(
                wide * source[...].astype(jnp.float32), axis=0, keepdims=True
            )

    def work_front(block):
        x = front[block]
        front_mixed[...] = (
            x.astype(jnp.float32) * taps[0:1, :]
            + mm(shifts[0], x) * taps[1:2, :]
            + mm(shifts[1], x) * taps[2:3, :]
        ).astype(jnp.bfloat16)
        total[...] = jnp.zeros_like(total)

        def part(f, carry):
            there = pl.ds(pl.multiple_of(f * PART, PART), PART)
            pre_act = mm(front_mixed[...], up[:, there])
            hidden = gelu_parts(pre_act)[0].astype(jnp.bfloat16)
            total[...] += mm(hidden, down[there, :])
            return carry

        lax.fori_loop(0, width // PART, part, 0)
        for t in range(tiles):
            weight = widen(weights_front[block, me, t : t + 1, :], channels)
            here = slice(t * steps, (t + 1) * steps)
            expert_rows = total[here, :].astype(jnp.bfloat16).astype(jnp.float32)
            results[block, here, :] = (weight * expert_rows).astype(jnp.bfloat16)

    def give_turn(at, outward):
        pl.semaphore_signal(
            turns.at[at],
            inc=1,
            device_id={"phase": 1 - phase, "expert": me - outward},
            device_id_type=MESH,
        )

    def last_block(block, k):
        return block == (n - 1) * (1 - k % 2)

    def back_arrived(block, k, half, outward):
        @pl.when((phase == half) & last_block(block, k))
        def _():
            give_turn(1 - k % 2, outward)

    def front_arrived(block, k, half, outward):
        if half == 0:
            @pl.when((phase == 0) & last_block(block, k))
            def _():
                give_turn(3 - k % 2, outward)

    def await_turn(first, send):
        for i in (0, 1):
            direction = (i + me // (n // 2)) % 2

            @pl.when(within(n, me + 1 - 2 * direction))
            def _():
                pl.semaphore_wait(turns.at[first + direction], 1)

            send(direction)

    def back_step(k, carry):
        distance = (k + 1) // 2
        block = place(me, k)

        @pl.when(within(n, block))
        def _():
            work_back(block)
            home_first(n, me, k, back_home)

        @pl.when(k == 0)
        def _():
            @pl.when(phase == 1)
            def _():
                work_front(me)
                await_turn(0, lambda direction: own_send(n, me, direction, *back_way))

            take_ring(n, me, 1, 0, back_way, back_arrived)
            take_ring(n, me, 1, 1, back_way, back_arrived)

        @pl.when((k == 0) & (phase == 0) & edge)
        def _():
            for direction in (0, 1):
                own_send(n, me, direction, *front_way)

        @pl.when(k % 2 == 1)
        def _():
            take_ring(n, me, distance + 1, 0, back_way, back_arrived)

        @pl.when((k % 2 == 0) & (k > 0))
        def _():
            take_ring(n, me, distance + 1, 1, back_way, back_arrived)

        return carry

    lax.fori_loop(0, 2 * n - 1, back_step, 0)

    def down_rows(piece, dest):
        def rows_of(i, carry):
            extent = down_land.shape[1]
            there = pl.ds(pl.multiple_of(dest * extent + i * 256, 256), 256)
            here = pl.ds(pl.multiple_of(i * 256, 256), 256)
            down_part[piece, here, :] = mm(hidden[:, there], grads[...], ((0,), (0,))).astype(jnp.bfloat16)
            return carry

        lax.fori_loop(0, down_land.shape[1] // 256, rows_of, 0)

    def up_rows(piece, dest):
        def rows_of(i, carry):
            extent = up_land.shape[1]
            there = pl.ds(pl.multiple_of(dest * extent + i * 256, 256), 256)
            here = pl.ds(pl.multiple_of(i * 256, 256), 256)
            up_part[piece, here, :] = mm(mixed[:, there], pre_grads[...], ((0,), (0,))).astype(jnp.bfloat16)
            return carry

        lax.fori_loop(0, up_land.shape[1] // 256, rows_of, 0)

    def share(part, land, sends, recvs, slot, target):
        return pltpu.make_async_remote_copy(
            src_ref=part.at[slot],
            dst_ref=land.at[slot],
            send_sem=sends.at[slot],
            recv_sem=recvs.at[slot],
            device_id={"dp": target},
            device_id_type=MESH,
        )

    def pass_on(part, land, sends, recvs, target):
        return pltpu.make_async_remote_copy(
            src_ref=part.at[2],
            dst_ref=land.at[2],
            send_sem=sends.at[2],
            recv_sem=recvs.at[2],
            device_id={"dp": target},
            device_id_type=MESH,
        )

    def relay(part, land, copies, hop):
        copies[0].wait_recv()

        def add(i, carry):
            there = pl.ds(pl.multiple_of(i * CHUNK, CHUNK), CHUNK)
            part[2, there, :] = (
                land[0, there, :].astype(jnp.float32) + part[2, there, :].astype(jnp.float32)
            ).astype(jnp.bfloat16)
            return carry

        lax.fori_loop(0, land.shape[1] // CHUNK, add, 0)
        hop.start()

    def arrive(part, land, copies, hop, out, sem):
        copies[1].wait_recv()
        hop.wait_recv()

        def add(i, carry):
            there = pl.ds(pl.multiple_of(i * CHUNK, CHUNK), CHUNK)
            summed = (
                part[3, there, :].astype(jnp.float32)
                + land[1, there, :].astype(jnp.float32)
                + land[2, there, :].astype(jnp.float32)
            )
            part[3, there, :] = (summed * grad_scale).astype(jnp.bfloat16)
            return carry

        lax.fori_loop(0, land.shape[1] // CHUNK, add, 0)
        store = pltpu.make_async_copy(part.at[3], out, sem)
        store.start()
        return store

    down_copies = [
        share(down_part, down_land, down_send, down_recv, 0, y_lane),
        share(down_part, down_land, down_send, down_recv, 1, y_lane),
    ]
    up_copies = [
        share(up_part, up_land, up_send, up_recv, 0, x_lane),
        share(up_part, up_land, up_send, up_recv, 1, x_lane),
    ]
    down_rows(0, far_lane)
    down_copies[0].start()
    up_rows(0, far_lane)
    up_copies[0].start()
    down_rows(1, y_lane)
    down_copies[1].start()
    up_rows(1, x_lane)
    up_copies[1].start()
    tap_copies = [
        pltpu.make_async_remote_copy(
            src_ref=taps_grad.at[pl.ds(0, 8), pl.ds(pl.multiple_of(peer * tap_share, tap_share), tap_share)],
            dst_ref=taps_land.at[j],
            send_sem=taps_send.at[j],
            recv_sem=taps_recv.at[j],
            device_id={"dp": peer},
            device_id_type=MESH,
        )
        for tap_share in (taps_land.shape[2],)
        for j, peer in enumerate(peers)
    ]
    for copy in tap_copies:
        copy.start()

    down_rows(2, x_lane)
    up_rows(2, y_lane)
    down_hop = pass_on(down_part, down_land, down_send, down_recv, x_lane)
    up_hop = pass_on(up_part, up_land, up_send, up_recv, y_lane)
    down_rows(3, lane)
    up_rows(3, lane)
    relay(down_part, down_land, down_copies, down_hop)
    relay(up_part, up_land, up_copies, up_hop)
    home_rest(n, me, back_home)

    @pl.when(phase == 0)
    def _():
        def send(direction):
            @pl.when(jnp.logical_not(edge))
            def _():
                own_send(n, me, direction, *front_way)

        await_turn(0, send)

    @pl.when(phase == 1)
    def _():
        await_turn(2, lambda direction: own_send(n, me, direction, *front_way))

    def front_step(k, carry):
        distance = (k + 1) // 2
        block = place(me, k)

        @pl.when(within(n, block) & ((k > 0) | (phase == 0)))
        def _():
            work_front(block)
            home_first(n, me, k, front_home)

        @pl.when(k == 0)
        def _():
            take_ring(n, me, 1, 0, front_way, front_arrived)
            take_ring(n, me, 1, 1, front_way, front_arrived)

        @pl.when(k % 2 == 1)
        def _():
            take_ring(n, me, distance + 1, 0, front_way, front_arrived)

        @pl.when((k % 2 == 0) & (k > 0))
        def _():
            take_ring(n, me, distance + 1, 1, front_way, front_arrived)

        return carry

    lax.fori_loop(0, 2 * n - 1, front_step, 0)

    def settle(way, resid, out):
        source, landing = way[:2]
        for dir_index in (0, 1):
            behind = me - (1 - 2 * dir_index)

            @pl.when(within(n, behind))
            def _():
                for half in range(HALVES):
                    home_copy(dir_index, half, *way, me, behind).wait_recv()

        out[...] = resid.astype(jnp.float32) + source[me].astype(jnp.float32)
        for dir_index in (0, 1):
            behind = me - (1 - 2 * dir_index)

            @pl.when((behind >= 0) & (behind < n))
            def _():
                out[...] += landing[dir_index, me].astype(jnp.float32)

    def swap(source):
        return pltpu.make_async_remote_copy(
            src_ref=source,
            dst_ref=passed_hbm,
            send_sem=swap_sems.at[0],
            recv_sem=swap_sems.at[1],
            device_id={"phase": 1 - phase},
            device_id_type=MESH,
        )

    def finish(source):
        return pltpu.make_async_copy(source, finished_hbm, local_sems.at[7])

    settle(back_home, incoming[me], total)
    out_back[...] = total[...].astype(jnp.bfloat16)

    @pl.when(phase == 0)
    def _():
        finish(out_back).start()

    @pl.when(phase == 1)
    def _():
        swap(out_back).start()

    stores = [
        arrive(down_part, down_land, down_copies, down_hop, down_grad_hbm, local_sems.at[5]),
        arrive(up_part, up_land, up_copies, up_hop, up_grad_hbm, local_sems.at[6]),
    ]
    for copy in tap_copies:
        copy.wait()
    tap_share = taps_land.shape[2]
    taps_sum = taps_grad[:, pl.ds(pl.multiple_of(lane * tap_share, tap_share), tap_share)]
    for j in range(ndp - 1):
        taps_sum = taps_sum + taps_land[j]
    taps_out_ref[...] = taps_sum * grad_scale
    home_rest(n, me, front_home)
    settle(front_home, front[me], total)
    out_front[...] = total[...].astype(jnp.bfloat16)

    @pl.when(phase == 0)
    def _():
        swap(out_front).start()

    @pl.when(phase == 1)
    def _():
        finish(out_front).start()

    drain_gather(n, me, *back_way)
    drain_gather(n, me, *front_way)
    home_sent(n, me, back_home)
    home_sent(n, me, front_home)
    for copy in down_copies + up_copies + [down_hop, up_hop]:
        copy.wait_send()
    for store in stores:
        store.wait()

    @pl.when(phase == 0)
    def _():
        finish(out_back).wait()

    @pl.when(phase == 1)
    def _():
        finish(out_front).wait()

    swap(out_front).wait()


def deliver_kernel(*refs):
    count = len(refs) // 2
    for i in range(count - 1):
        refs[count + i][...] = refs[i][...]
    taps_in, taps_out = refs[count - 1], refs[-1]
    taps_out[0, 0] = taps_in[: taps_out.shape[2], :]


def local_gather(
    fwd_in, saved_in, upstream, routes, gates, capacity, dilation_log, conv_kernel,
    up_weight, down_weight,
):
    n = lax.axis_size("expert")
    ndp = lax.axis_size("dp")
    _, tiles, steps, channels = fwd_in.shape
    width = up_weight.shape[3]
    rows = tiles * steps
    flat, every = (rows, channels), (n, rows, channels)
    bf16, f32 = jnp.bfloat16, jnp.float32
    vmem, anywhere = pl.BlockSpec(memory_space=pltpu.VMEM), pl.BlockSpec(memory_space=pl.ANY)
    smem = pl.BlockSpec(memory_space=pltpu.SMEM)
    slots = 2 * n + 1
    up_share, down_share, tap_share = channels // ndp, width // ndp, channels // ndp
    dma = pltpu.SemaphoreType.DMA
    out_shape = (
        jax.ShapeDtypeStruct(flat, bf16),
        jax.ShapeDtypeStruct(flat, bf16),
        jax.ShapeDtypeStruct((up_share, width), bf16),
        jax.ShapeDtypeStruct((down_share, channels), bf16),
        jax.ShapeDtypeStruct((8, tap_share), f32),
    )
    outs = pl.pallas_call(
        functools.partial(step_kernel, n, ndp, tiles, steps),
        out_shape=out_shape,
        in_specs=[anywhere] * 3 + [smem] * 4 + [vmem, anywhere, anywhere],
        out_specs=(anywhere, anywhere, anywhere, anywhere, vmem),
        scratch_shapes=[
            pltpu.VMEM(every, bf16),
            pltpu.VMEM(every, bf16),
            pltpu.VMEM(every, bf16),
            pltpu.VMEM((n, n, tiles, LANES), f32),
            pltpu.VMEM((n, n, tiles, LANES), f32),
            pltpu.VMEM((4, rows, rows), bf16),
            pltpu.VMEM((8, channels), f32),
            pltpu.VMEM((channels, width), bf16),
            pltpu.VMEM((width, channels), bf16),
            pltpu.VMEM((n * rows, channels), bf16),
            pltpu.VMEM((n * rows, channels), bf16),
            pltpu.VMEM((n * rows, width), bf16),
            pltpu.VMEM((n * rows, width), bf16),
            pltpu.VMEM(flat, bf16),
            pltpu.VMEM(flat, bf16),
            pltpu.VMEM(flat, f32),
            pltpu.VMEM(every, bf16),
            pltpu.VMEM((ndp, up_share, width), bf16),
            pltpu.VMEM(every, bf16),
            pltpu.VMEM((2,) + every, bf16),
            pltpu.VMEM((2,) + every, bf16),
            pltpu.VMEM((ndp, down_share, channels), bf16),
            pltpu.VMEM((3, up_share, width), bf16),
            pltpu.VMEM((3, down_share, channels), bf16),
            pltpu.VMEM((8, channels), f32),
            pltpu.VMEM((ndp - 1, 8, tap_share), f32),
            dma((8,)),
            dma((slots, HALVES, 3)),
            dma((slots, HALVES, 3)),
            dma((slots, HALVES, 2)),
            dma((slots, HALVES, 2)),
            dma((n, HALVES)),
            dma((2, n, HALVES)),
            dma((n, HALVES)),
            dma((2, n, HALVES)),
            dma((3,)),
            dma((3,)),
            dma((3,)),
            dma((3,)),
            dma((ndp - 1,)),
            dma((ndp - 1,)),
            dma((2,)),
            pltpu.SemaphoreType.REGULAR((4,)),
        ],
        compiler_params=pltpu.CompilerParams(
            collective_id=0, has_side_effects=True, vmem_limit_bytes=VMEM_BYTES
        ),
    )(
        fwd_in.reshape(flat), saved_in.reshape(flat), upstream.reshape(flat),
        routes[0].transpose(0, 2, 1), gates[0].transpose(0, 2, 1), capacity,
        dilation_log, conv_kernel[0, 0], up_weight[0, 0], down_weight[0, 0],
    )
    pieces = [
        pl.BlockSpec((out.shape[0] // 2, out.shape[1]), lambda i: (i, 0)) for out in out_shape[:4]
    ]
    taps_shape = jax.ShapeDtypeStruct((1, 1, TAPS, tap_share), f32)
    passed, finished, up_grad, down_grad, taps_out = pl.pallas_call(
        deliver_kernel,
        grid=(2,),
        out_shape=out_shape[:4] + (taps_shape,),
        in_specs=pieces + [pl.BlockSpec(out_shape[4].shape, lambda i: (0, 0))],
        out_specs=tuple(pieces) + (pl.BlockSpec(taps_shape.shape, lambda i: (0, 0, 0, 0)),),
    )(*outs)
    shape = fwd_in.shape
    return (
        passed.reshape(shape),
        finished.reshape(shape),
        up_grad[None, None],
        down_grad[None, None],
        taps_out,
    )


def local(*operands):
    tile_count, experts = operands[0].shape[1], operands[5].shape[1]
    slot_total = experts * 2 * max(1, (tile_count * TOP + experts - 1) // experts)
    gathers = experts * tile_count <= slot_total and lax.axis_size("dp") == 4
    return local_gather(*operands) if gathers else local_slots(*operands)


def solution(mesh):
    return jax.shard_map(
        local,
        mesh=mesh,
        in_specs=(
            P("phase", ("expert", "dp"), None, None),
            P("phase", ("expert", "dp"), None, None),
            P("phase", ("expert", "dp"), None, None),
            P("phase", None, ("expert", "dp"), None),
            P("phase", None, ("expert", "dp"), None),
            P("phase", None),
            P("phase", None),
            P("phase", "expert", None, None),
            P("phase", "expert", None, None),
            P("phase", "expert", None, None),
        ),
        out_specs=(
            P("phase", ("expert", "dp"), None, None),
            P("phase", ("expert", "dp"), None, None),
            P("phase", "expert", "dp", None),
            P("phase", "expert", "dp", None),
            P("phase", "expert", None, "dp"),
        ),
        check_vma=False,
    )
```
